128 devices in a mesh: section: 8 (over z_hi, x), tile: 16 (over z_lo, y, core).
Axes of the slice: x: 4, y: 4, z: 4 (z_hi: 2, z_lo: 2; z = z_hi * 2 + z_lo), core: 2. Of those that a mesh axis runs over, the one named last changes fastest.
Arguments:
- activations: bfloat16 [16, 16, 16, 16, 256], P('section', 'tile'), may hold values from -6 to 6
- weight: bfloat16 [8, 9, 256, 256], P('section'), may hold values from -0.125 to 0.125
- conv_bias: bfloat16 [8, 256], P('section'), may hold values from -3 to 3
- norm_gain: bfloat16 [8, 256], P('section'), may hold values from 0.099609375 to 1.8984375
- metric: bfloat16 [16, 9, 256], P('tile'), may hold values from 0.5 to 2
- neighbours: int32 [3, 16, 8], replicated, may hold values from 0 to 15, as said below
Outputs:
- advanced: bfloat16 [16, 16, 16, 16, 256], P('section', 'tile')
The draws below stay inside these ranges and needn't reach their ends.
Inputs may be any that keep to these rules, and one draw needn't show every extreme that they name: `neighbours`: row 0 names neighbour tiles; each of the 8 columns names every tile once. Row 1 is a side or corner number 0 to 3. Row 2 is 0 or 1 for the 4 side columns and 0 for the corner columns.
All inputs are finite; a program needn't handle non-finite values.
Results may differ from the reference program's by a relative error of at most 0.0075.
Values may be sent and summed in bfloat16 or wider, within the bound.
A program may use at most 64 MiB of HBM per device.

```python
import math
import jax
import jax.numpy as jnp
from jax import lax

C = 256
SIDE = 16
TILES = 16
MICRO = 16
N_SECTION = 8


def draw_neighbours(key, part):
    key_tiles = jax.random.fold_in(key, 11)
    key_sides = jax.random.fold_in(key, 12)
    key_flips = jax.random.fold_in(key, 13)
    columns = [jax.random.permutation(jax.random.fold_in(key_tiles, column), TILES).astype(jnp.int32) for column in range(8)]
    tile_rows = jnp.stack(columns, axis=1)
    side_rows = jax.random.randint(key_sides, (TILES, 8), 0, 4).astype(jnp.int32)
    flip_sides = jax.random.randint(key_flips, (TILES, 4), 0, 2).astype(jnp.int32)
    flip_rows = jnp.concatenate([flip_sides, jnp.zeros((TILES, 4), jnp.int32)], axis=1)
    return jnp.stack([tile_rows, side_rows, flip_rows], axis=0)


def level_of(key, extent, cuts, least, top_value):
    def one(dim, shards_of):
        heights = jax.random.uniform(jax.random.fold_in(jax.random.fold_in(key, 6), dim), (shards_of,), jnp.float32, least / len(cuts), top_value / len(cuts))
        return jnp.repeat(jnp.exp(heights), extent[dim] // shards_of).reshape((-1,) + (1,) * (len(extent) - dim - 1))

    factor_of = one(*cuts[0])
    for cut in cuts[1:]:
        factor_of = factor_of * one(*cut)
    return factor_of


def noise(stream_key, dims, deviation, bound, cuts=(), kind=jnp.bfloat16):
    drawn = deviation * jax.random.normal(stream_key, dims, jnp.float32)
    if cuts:
        drawn = drawn * level_of(stream_key, dims, cuts, -0.22, 0.18)
    return jnp.clip(drawn, -bound, bound).astype(kind)


def setup_inputs(seed: int = 0) -> dict:
    key_of = jax.random.split(jax.random.key(seed), 7)
    return {
        "activations": noise(key_of[0], (MICRO, TILES, SIDE, SIDE, C), 1.0, 6.0, ((0, 8), (1, 16))),
        "weight": noise(key_of[1], (N_SECTION, 9, C, C), (9 * C) ** -0.5, 0.125, ((0, 8),)),
        "conv_bias": noise(key_of[2], (N_SECTION, C), 0.5, 3.0, ((0, 8),)),
        "norm_gain": jnp.clip(1.0 + 0.18 * jax.random.normal(key_of[3], (N_SECTION, C), jnp.float32), 0.099609375, 1.8984375).astype(jnp.bfloat16),
        "metric": jnp.clip(jnp.exp(math.log(2.0) - 1.3862944 * jax.random.uniform(key_of[4], (TILES, 9, SIDE * SIDE), jnp.float32) ** level_of(key_of[4], (TILES, 9, SIDE * SIDE), ((0, 16),), -0.2, 0.2)), 0.5, 2.0).astype(jnp.bfloat16),
        "neighbours": draw_neighbours(jax.random.fold_in(key_of[6], 71), 0),
    }


def normalize(states, gain_row):
    values = states.astype(jnp.float32)
    mean_sq = lax.optimization_barrier(jnp.mean(values * values, axis=-1, keepdims=True))
    return (values * lax.rsqrt(mean_sq + 1e-05) * gain_row.astype(jnp.float32)).astype(jnp.bfloat16)

def side_strips(normed):
    side_len = normed.shape[1]
    return jnp.stack([normed[:, 0], normed[:, :, side_len - 1], normed[:, side_len - 1], normed[:, :, 0]], axis=1)

def assemble(normed, strips, corners):
    top_row = jnp.concatenate([corners[0][:, None], strips[0], corners[1][:, None]], axis=1)
    middle = jnp.concatenate([strips[3][:, :, None], normed, strips[1][:, :, None]], axis=2)
    bottom = jnp.concatenate([corners[3][:, None], strips[2], corners[2][:, None]], axis=1)
    return jnp.concatenate([top_row[:, None], middle, bottom[:, None]], axis=1)

def convolve(padded, weight_taps, metric_taps, side_len):
    count = padded.shape[0]
    channels = padded.shape[-1]
    total = jnp.zeros((count, side_len * side_len, channels), jnp.float32)
    for row_off in range(3):
        for col_off in range(3):
            tap_index = row_off * 3 + col_off
            shifted = padded[:, row_off:row_off + side_len, col_off:col_off + side_len, :].reshape(-1, channels)
            product = jnp.dot(shifted, weight_taps[tap_index], preferred_element_type=jnp.float32)
            product = product.reshape(count, side_len * side_len, channels)
            total = total + product * metric_taps[:, tap_index, :, None].astype(jnp.float32)
    return total

def apply_layer(states, weight_taps, bias_row, gain_row, metric, neighbours):
    side_len = states.shape[1]
    channels = states.shape[-1]
    normed = normalize(states, gain_row)
    borders = side_strips(normed)
    strips = []
    for side_index in range(4):
        source = neighbours[0, :, side_index]
        which = neighbours[1, :, side_index]
        strip_rows = borders[source, which]
        strip_rows = jnp.where((neighbours[2, :, side_index] == 1)[:, None, None], strip_rows[:, ::-1], strip_rows)
        strips.append(strip_rows)
    corners = []
    for corner_index in range(4):
        source = neighbours[0, :, 4 + corner_index]
        which = neighbours[1, :, 4 + corner_index]
        rim_index = jnp.where(which < 2, 0, 2).astype(jnp.int32)
        position = jnp.where((which == 1) | (which == 2), side_len - 1, 0).astype(jnp.int32)
        corners.append(borders[source, rim_index, position])
    padded = assemble(normed, strips, corners)
    conv = convolve(padded, weight_taps, metric, side_len)
    conv = conv.reshape(states.shape)
    result = states.astype(jnp.float32) + jax.nn.silu(conv + bias_row.astype(jnp.float32))
    return result.astype(jnp.bfloat16)

def reference(activations, weight, conv_bias, norm_gain, metric, neighbours):
    sections = weight.shape[0]
    per_home = activations.shape[0] // sections
    homes = (jnp.arange(activations.shape[0]) // per_home).astype(jnp.int32)

    def one_micro(inputs):
        states, home_section = inputs
        for section_step in range(sections):
            layer_id = ((home_section + section_step) % sections).astype(jnp.int32)
            states = apply_layer(states, weight[layer_id], conv_bias[layer_id], norm_gain[layer_id], metric, neighbours)
        return states
    return lax.map(one_micro, (activations, homes))
```

```python
import jax
import jax.numpy as jnp
from jax import lax
from jax.experimental import pallas as pl
from jax.experimental.pallas import tpu as pltpu
from jax.sharding import PartitionSpec as P

MESH = pl.DeviceIdType.MESH
C = 256
HALF = 9 * C // 2
F32, BF16 = jnp.float32, jnp.bfloat16
PITCH = 18


def rcopy(src, dst, send, recv, device):
    return pltpu.make_async_remote_copy(
        src_ref=src, dst_ref=dst, send_sem=send, recv_sem=recv, device_id=device, device_id_type=MESH
    )


def kernel(
    nb, act, weight, metric, bias, gain, out,
    W, V, Z, rim_a, rim_b, metr, MB, BG, bgs, PM, pad,
    act_s, act_r, met_s, met_r, w_s, w_r, bg_s, bg_r, x_s, x_r,
    rim_s, rim_r, out_s, out_r, loc, go,
):
    s, t = lax.axis_index("section"), lax.axis_index("tile")
    hi, x = s // 4, lax.rem(s, 4)
    zl, y, c = t // 8, lax.rem(t // 2, 4), lax.rem(t, 2)
    even = lax.rem(y, 2) == 0
    active = jnp.logical_and(zl == 1, even)
    relay = jnp.logical_and(zl == 1, jnp.logical_not(even))
    cross1 = jnp.logical_and(zl == 0, even)
    cross2 = jnp.logical_and(zl == 0, jnp.logical_not(even))

    def sec(h, xx):
        return h * 4 + lax.rem(xx + 8, 4)

    def tid(plane, row, core):
        return plane * 8 + 2 * lax.rem(row + 4, 4) + core

    partner = (s, t + 1 - 2 * c)
    homes = [(s, 8 + zl), (s, 12 + zl)]
    is_home = [t == 8 + zl, t == 12 + zl]

    f1_dst = [(sec(hi, x - 1), t), (sec(hi, x + 1), t)]
    f2_dst = (sec(hi, x + 2), tid(1, y - 1, c))
    e3_dst = (sec(1 - hi, x + 1), tid(1, y + 1, c))
    e0_dst = (sec(1 - hi, x), tid(1, y + 1, c))
    e1_dst = (sec(1 - hi, x - 1), tid(1, y, c))
    e2_dst = (sec(1 - hi, x + 2), tid(1, y - 1, c))
    e0_src = (sec(1 - hi, x), tid(1, y - 1, c))
    e3_src = (sec(1 - hi, x - 1), tid(1, y - 1, c))
    w_src = [
        (sec(hi, x + 1), t), (sec(hi, x - 1), t), (sec(hi, x + 2), tid(1, y + 1, c)), e0_src, e3_src,
        (sec(1 - hi, x + 1), tid(0, y, c)), (sec(1 - hi, x + 2), tid(0, y + 1, c)),
    ]

    barrier = pltpu.get_barrier_semaphore()

    def hello(device):
        pl.semaphore_signal(barrier, inc=1, device_id=device, device_id_type=MESH)

    for j in range(2):
        @pl.when(jnp.logical_not(is_home[j]))
        def _():
            hello(homes[j])

    @pl.when(active)
    def _():
        for i in range(8):
            @pl.when(t != c * 8 + i)
            def _():
                hello((s, c * 8 + i))
        for d in w_src:
            hello(d)
        hello(partner)

    @pl.when(relay)
    def _():
        for d in (f2_dst, e3_dst, e0_dst):
            hello(d)

    @pl.when(cross1)
    def _():
        hello(e1_dst)

    @pl.when(cross2)
    def _():
        hello(e2_dst)

    at_home = jnp.logical_or(is_home[0], is_home[1])
    greeted = jnp.where(at_home, 1, 2) + jnp.where(relay, 3, jnp.where(active, jnp.where(c == zl, 15, 16), 1))
    pl.semaphore_wait(barrier, greeted)

    slot = lax.rem(t, 8)
    for j in range(2):
        @pl.when(is_home[j])
        def _():
            pltpu.make_async_copy(metric.at[0], metr.at[slot], met_r.at[slot]).start()
            pltpu.make_async_copy(act.at[j], V.at[slot], act_r.at[slot]).start()

        @pl.when(jnp.logical_not(is_home[j]))
        def _():
            rcopy(metric.at[0], metr.at[slot], met_s.at[j], met_r.at[slot], homes[j]).start()
            rcopy(act.at[j], V.at[slot], act_s.at[j], act_r.at[slot], homes[j]).start()

    bgs[0:8] = jnp.broadcast_to(bias[...], (8, C))
    bgs[8:16] = jnp.broadcast_to(gain[...], (8, C))

    mine = pl.ds(pl.multiple_of(c * HALF, HALF), HALF)

    def stream(device, n):
        k = lax.rem(s - device[0] + 8, 8)
        return rcopy(weight.at[mine], W.at[k, mine], w_s.at[n], w_r.at[k], device)

    def begin(device, n):
        stream(device, n).start()

    def sent(device, n):
        stream(device, n).wait_send()

    def lines(device, n):
        k = lax.rem(s - device[0] + 8, 8)
        return rcopy(bgs, BG.at[k], bg_s.at[n], bg_r.at[k], device)

    def tell(devices):
        for n, d in enumerate(devices):
            lines(d, n).start()

    def told(devices):
        for n, d in enumerate(devices):
            lines(d, n).wait_send()

    def arrived(k):
        rcopy(weight.at[mine], W.at[k, mine], w_s.at[0], w_r.at[k], partner).wait_recv()

    @pl.when(relay)
    def _():
        tell((f2_dst, e3_dst, e0_dst))

        @pl.when(x >= 2)
        def _():
            begin(f2_dst, 0)
        pl.semaphore_wait(go, 2)
        begin(e3_dst, 1)
        sent(e3_dst, 1)
        begin(e0_dst, 2)
        sent(e0_dst, 2)

        @pl.when(x < 2)
        def _():
            begin(f2_dst, 0)
        sent(f2_dst, 0)
        told((f2_dst, e3_dst, e0_dst))

    @pl.when(cross1)
    def _():
        tell((e1_dst,))
        begin(e1_dst, 0)
        sent(e1_dst, 0)
        told((e1_dst,))

    @pl.when(cross2)
    def _():
        tell((e2_dst,))
        begin(e2_dst, 0)
        sent(e2_dst, 0)
        told((e2_dst,))

    @pl.when(active)
    def _():
        tell(f1_dst)
        for n, d in enumerate(f1_dst):
            begin(d, n)
        own_w = pltpu.make_async_copy(weight, W.at[0], loc.at[0])
        own_w.start()
        BG[0] = bgs[...]

        @pl.loop(0, 8)
        def _(i):
            g = c * 8 + i
            row = lax.broadcasted_iota(jnp.int32, (16, 128), 0)
            col = lax.broadcasted_iota(jnp.int32, (16, 128), 1)
            for side in range(4):
                flip = nb[2, g, side]
                want = side * 16 + row + flip * (15 - 2 * row)
                PM[i, side * 16:side * 16 + 16, :] = jnp.where(col == want, 1.0, 0.0).astype(BF16)
            want = jnp.zeros((16, 128), jnp.int32) - 1
            for corner in range(4):
                which = nb[1, g, 4 + corner]
                last = 15 * (((which + 1) >> 1) & 1)
                want = jnp.where(row == corner, 64 + corner * 16 + last, want)
            PM[i, 64:80, :] = jnp.where(col == want, 1.0, 0.0).astype(BF16)

        @pl.loop(0, 8)
        def _(i):
            rcopy(metric.at[0], metr.at[i], met_s.at[0], met_r.at[i], partner).wait_recv()
            for q in range(9):
                line = jnp.broadcast_to(metr[i, q:q + 1, :].astype(F32), (128, C))
                MB[i, q] = line.T.astype(BF16)

        def normed(values, k):
            mean_sq = jnp.mean(values * values, axis=-1, keepdims=True)
            return (values * lax.rsqrt(mean_sq + 1e-05) * BG[k, 8:9, :].astype(F32)).astype(BF16)

        def keep_rim(i, rim, z):
            g = c * 8 + i
            cube = z.astype(F32).reshape(16, 16, C)
            rim[4 * g] = z[0:16]
            rim[4 * g + 1] = cube[:, 15, :].astype(BF16)
            rim[4 * g + 2] = z[240:256]
            rim[4 * g + 3] = cube[:, 0, :].astype(BF16)

        def rim_copy(i, rim, par, who):
            own = pl.ds(4 * (who * 8 + i), 4)
            return rcopy(rim.at[own], rim.at[own], rim_s.at[par, i], rim_r.at[par, i], partner)

        @pl.loop(0, 8)
        def _(i):
            rcopy(act.at[0], V.at[i], act_s.at[0], act_r.at[i], partner).wait_recv()
            z = normed(V[i].astype(F32), 0)
            Z[i] = z
            keep_rim(i, rim_a, z)
            rim_copy(i, rim_a, 0, c).start()

        for d in (e0_src, e3_src):
            pl.semaphore_signal(go, inc=1, device_id=d, device_id_type=MESH)
        own_w.wait()
        for k in range(1, 8):
            rcopy(bgs, BG.at[k], bg_s.at[0], bg_r.at[k], partner).wait_recv()

        def exchange(k):
            return rcopy(W.at[k, mine], W.at[k, mine], x_s.at[k], x_r.at[k], partner)

        other = pl.ds(pl.multiple_of((1 - c) * HALF, HALF), HALF)

        def out_copy(i):
            g = c * 8 + i
            micro = y // 2
            return rcopy(V.at[i], out.at[micro], out_s.at[i], out_r.at[micro], (s, g))

        def own_copy(i):
            micro = y // 2
            return pltpu.make_async_copy(V.at[i], out.at[micro], out_r.at[micro])

        def tile_step(i, k, rim_in, rim_out, par_out):
            g = c * 8 + i
            pieces = []
            for side in range(4):
                pieces.append(rim_in[4 * nb[0, g, side] + nb[1, g, side]])
            for corner in range(4, 8):
                pieces.append(rim_in[4 * nb[0, g, corner] + (nb[1, g, corner] & 2)])
            frame = jnp.dot(PM[i], jnp.concatenate(pieces, axis=0), preferred_element_type=F32)
            z = Z[i].astype(F32)
            for h in range(2):
                lanes = slice(h * 128, h * 128 + 128)
                f, zh = frame[:, lanes], z[:, lanes]
                pad[h, 1:17, :] = f[0:16]
                pad[h, pl.ds(PITCH + 17, 16, stride=PITCH), :] = f[16:32]
                pad[h, 17 * PITCH + 1:17 * PITCH + 17, :] = f[32:48]
                pad[h, pl.ds(PITCH, 16, stride=PITCH), :] = f[48:64]
                pad[h, 0:1, :] = f[64:65]
                pad[h, 17:18, :] = f[65:66]
                pad[h, 17 * PITCH + 17:17 * PITCH + 18, :] = f[66:67]
                pad[h, 17 * PITCH:17 * PITCH + 1, :] = f[67:68]
                for r in range(16):
                    pad[h, (r + 1) * PITCH + 1:(r + 1) * PITCH + 17, :] = zh[r * 16:r * 16 + 16]
            total = None
            for b in range(3):
                shifted = [
                    jnp.concatenate(
                        [pad[h, r * PITCH + b:r * PITCH + b + 16, :].astype(BF16) for r in range(18)], axis=0
                    )
                    for h in range(2)
                ]
                for a in range(3):
                    q = 3 * a + b
                    lhs = jnp.concatenate([sh[a * 16:a * 16 + 256] * MB[i, q] for sh in shifted], axis=1)
                    part = jnp.dot(lhs, W[k, q * C:q * C + C, :], preferred_element_type=F32)
                    total = part if total is None else total + part
            half = 0.5 * (total + BG[k, 0:1, :].astype(F32))
            v = (V[i].astype(F32) + half + half * jnp.tanh(half)).astype(BF16)
            V[i] = v

            @pl.when(k < 7)
            def _():
                nz = normed(v.astype(F32), lax.rem(k + 1, 8))
                Z[i] = nz
                keep_rim(i, rim_out, nz)
                rim_copy(i, rim_out, par_out, c).start()

            @pl.when(k == 7)
            def _():
                @pl.when(t == g)
                def _():
                    own_copy(i).start()

                @pl.when(t != g)
                def _():
                    out_copy(i).start()

        def layer(k, rim_in, par_in, rim_out, par_out):
            for i in range(8):
                rim_copy(i, rim_in, par_in, 1 - c).wait_recv()

            @pl.when(k > 0)
            def _():
                rcopy(W.at[k, other], W.at[k, other], x_s.at[k], x_r.at[k], partner).wait_recv()

            @pl.loop(0, 4)
            def _(i):
                tile_step(i, k, rim_in, rim_out, par_out)

            @pl.when(k < 7)
            def _():
                arrived(k + 1)
                exchange(k + 1).start()

            @pl.loop(4, 8)
            def _(i):
                tile_step(i, k, rim_in, rim_out, par_out)

        @pl.loop(0, 4)
        def _(n):
            @pl.when(n > 0)
            def _():
                for i in range(8):
                    rim_copy(i, rim_b, 1, c).wait_send()
            layer(2 * n, rim_a, 0, rim_b, 1)
            for i in range(8):
                rim_copy(i, rim_a, 0, c).wait_send()
            layer(2 * n + 1, rim_b, 1, rim_a, 0)

        for i in range(8):
            rim_copy(i, rim_b, 1, c).wait_send()
        for k in range(1, 8):
            exchange(k).wait_send()
        for n, d in enumerate(f1_dst):
            sent(d, n)
        told(f1_dst)
        for i in range(8):
            @pl.when(t != c * 8 + i)
            def _():
                out_copy(i).wait_send()

    for j in range(2):
        @pl.when(jnp.logical_not(is_home[j]))
        def _():
            rcopy(metric.at[0], metr.at[slot], met_s.at[j], met_r.at[slot], homes[j]).wait_send()
            rcopy(act.at[j], V.at[slot], act_s.at[j], act_r.at[slot], homes[j]).wait_send()
        rcopy(V.at[0], out.at[j], out_s.at[0], out_r.at[j], partner).wait_recv()


def local(activations, weight, conv_bias, norm_gain, metric, neighbours):
    anywhere = pl.BlockSpec(memory_space=pl.ANY)
    vmem = pl.BlockSpec(memory_space=pltpu.VMEM)
    dma = pltpu.SemaphoreType.DMA
    out = pl.pallas_call(
        kernel,
        name="sphere",
        out_shape=jax.ShapeDtypeStruct((2, C, C), BF16),
        in_specs=[pl.BlockSpec(memory_space=pltpu.SMEM), anywhere, anywhere, anywhere, vmem, vmem],
        out_specs=anywhere,
        scratch_shapes=[
            pltpu.VMEM((8, 9 * C, C), BF16),
            pltpu.VMEM((8, C, C), BF16),
            pltpu.VMEM((8, C, C), BF16),
            pltpu.VMEM((64, 16, C), BF16),
            pltpu.VMEM((64, 16, C), BF16),
            pltpu.VMEM((8, 9, C), BF16),
            pltpu.VMEM((8, 9, C, 128), BF16),
            pltpu.VMEM((8, 16, C), BF16),
            pltpu.VMEM((16, C), BF16),
            pltpu.VMEM((8, 80, 128), BF16),
            pltpu.VMEM((2, 336, 128), F32),
            dma((2,)), dma((8,)), dma((2,)), dma((8,)),
            dma((3,)), dma((8,)), dma((3,)), dma((8,)),
            dma((8,)), dma((8,)),
            dma((2, 8)), dma((2, 8)), dma((8,)), dma((2,)), dma((1,)),
            pltpu.SemaphoreType.REGULAR,
        ],
        compiler_params=pltpu.CompilerParams(collective_id=0, has_side_effects=True),
    )(
        neighbours,
        activations.reshape(2, C, C),
        weight.reshape(9 * C, C),
        metric,
        conv_bias,
        norm_gain,
    )
    return out.reshape(2, 1, 16, 16, C)


def solution(mesh):
    in_specs = (
        P("section", "tile", None, None, None),
        P("section", None, None, None),
        P("section", None),
        P("section", None),
        P("tile", None, None),
        P(),
    )
    out_specs = P("section", "tile", None, None, None)
    return jax.shard_map(local, mesh=mesh, in_specs=in_specs, out_specs=out_specs, check_vma=False)
```

```python
import jax
import jax.numpy as jnp
from jax import lax
from jax.experimental import pallas as pl
from jax.experimental.pallas import tpu as pltpu
from jax.sharding import PartitionSpec as P

MESH = pl.DeviceIdType.MESH
C = 256
HALF = 9 * C // 2
F32, BF16 = jnp.float32, jnp.bfloat16
PITCH = 18


def rcopy(src, dst, send, recv, device):
    return pltpu.make_async_remote_copy(
        src_ref=src, dst_ref=dst, send_sem=send, recv_sem=recv, device_id=device, device_id_type=MESH
    )


def kernel(
    nb, act, weight, metric, bias, gain, out,
    W, V, Z, rim_a, rim_b, metr, MB, BG, bgs, PM, pad,
    act_s, act_r, met_s, met_r, w_s, w_r, bg_s, bg_r, x_s, x_r,
    rim_s, rim_r, out_s, out_r, loc, hub_s, hub_r, go,
):
    s, t = lax.axis_index("section"), lax.axis_index("tile")
    hi, x = s // 4, lax.rem(s, 4)
    zl, y, c = t // 8, lax.rem(t // 2, 4), lax.rem(t, 2)
    even = lax.rem(y, 2) == 0
    active = jnp.logical_and(zl == 1, even)
    relay = jnp.logical_and(zl == 1, jnp.logical_not(even))
    cross1 = jnp.logical_and(zl == 0, even)
    cross2 = jnp.logical_and(zl == 0, jnp.logical_not(even))

    def sec(h, xx):
        return h * 4 + lax.rem(xx + 8, 4)

    def tid(plane, row, core):
        return plane * 8 + 2 * lax.rem(row + 4, 4) + core

    partner = (s, t + 1 - 2 * c)
    homes = [(s, 8 + zl), (s, 12 + zl)]
    is_home = [t == 8 + zl, t == 12 + zl]

    f1_dst = [(sec(hi, x - 1), t), (sec(hi, x + 1), t)]
    f2_dst = (sec(hi, x + 2), tid(1, y - 1, c))
    e3_dst = (sec(1 - hi, x + 1), tid(1, y + 1, c))
    hub_dst = (s, tid(1, y + 1, c))
    hub_src = (sec(1 - hi, x), tid(0, y, c))
    hub = (sec(1 - hi, x), tid(1, y, c))
    e1_dst = (sec(1 - hi, x - 1), tid(1, y, c))
    e2_dst = (sec(1 - hi, x + 2), tid(1, y - 1, c))
    e3_src = (sec(1 - hi, x - 1), tid(1, y - 1, c))
    w_src = [
        (sec(hi, x + 1), t), (sec(hi, x - 1), t), (sec(hi, x + 2), tid(1, y + 1, c)), (s, tid(1, y - 1, c)), e3_src,
        (sec(1 - hi, x + 1), tid(0, y, c)), (sec(1 - hi, x + 2), tid(0, y + 1, c)),
    ]

    barrier = pltpu.get_barrier_semaphore()

    def hello(device):
        pl.semaphore_signal(barrier, inc=1, device_id=device, device_id_type=MESH)

    for j in range(2):
        @pl.when(jnp.logical_not(is_home[j]))
        def _():
            hello(homes[j])

    @pl.when(active)
    def _():
        for i in range(8):
            @pl.when(t != c * 8 + i)
            def _():
                hello((s, c * 8 + i))
        for d in w_src:
            hello(d)
        hello(partner)

    @pl.when(relay)
    def _():
        for d in (f2_dst, e3_dst, hub_dst, hub_src):
            hello(d)

    @pl.when(cross1)
    def _():
        hello(e1_dst)

    @pl.when(cross2)
    def _():
        hello(e2_dst)
        hello(hub)

    at_home = jnp.logical_or(is_home[0], is_home[1])
    greeted = jnp.where(at_home, 1, 2) + jnp.where(relay, 4, jnp.where(active, jnp.where(c == zl, 15, 16), 1 + lax.rem(y, 2)))
    pl.semaphore_wait(barrier, greeted)

    def place(row, row0):
        rel = lax.rem(row - row0 + 4, 4)
        return jnp.where(rel == 0, 3, jnp.where(rel == 1, 1, jnp.where(rel == 2, 0, 2)))

    slots = [2 * place(y, 2 * j) + c for j in range(2)]
    for j in range(2):
        @pl.when(is_home[j])
        def _():
            pltpu.make_async_copy(metric.at[0], metr.at[slots[j]], met_r.at[slots[j]]).start()
            pltpu.make_async_copy(act.at[j], V.at[slots[j]], act_r.at[slots[j]]).start()

        @pl.when(jnp.logical_not(is_home[j]))
        def _():
            rcopy(metric.at[0], metr.at[slots[j]], met_s.at[j], met_r.at[slots[j]], homes[j]).start()
            rcopy(act.at[j], V.at[slots[j]], act_s.at[j], act_r.at[slots[j]], homes[j]).start()

    bgs[0:8] = jnp.broadcast_to(bias[...], (8, C))
    bgs[8:16] = jnp.broadcast_to(gain[...], (8, C))

    mine = pl.ds(pl.multiple_of(c * HALF, HALF), HALF)

    def stream(device, n):
        k = lax.rem(s - device[0] + 8, 8)
        return rcopy(weight.at[mine], W.at[k, mine], w_s.at[n], w_r.at[k], device)

    def begin(device, n):
        stream(device, n).start()

    def sent(device, n):
        stream(device, n).wait_send()

    def lines(device, n):
        k = lax.rem(s - device[0] + 8, 8)
        return rcopy(bgs, BG.at[k], bg_s.at[n], bg_r.at[k], device)

    def tell(devices):
        for n, d in enumerate(devices):
            lines(d, n).start()

    def told(devices):
        for n, d in enumerate(devices):
            lines(d, n).wait_send()

    def arrived(k):
        rcopy(weight.at[mine], W.at[k, mine], w_s.at[0], w_r.at[k], partner).wait_recv()

    PART = HALF // 4

    def hub_in(p):
        rows = pl.ds(pl.multiple_of(c * HALF + p * PART, 16), PART)
        return rcopy(weight.at[rows], W.at[4, rows], hub_s.at[p], hub_r.at[p], hub)

    def hub_on(p):
        rows = pl.ds(pl.multiple_of(c * HALF + p * PART, 16), PART)
        return rcopy(W.at[4, rows], W.at[4, rows], hub_s.at[p], w_r.at[4], hub_dst)

    @pl.when(relay)
    def _():
        tell((f2_dst, e3_dst))
        begin(f2_dst, 0)
        for p in range(4):
            hub_in(p).wait_recv()
            hub_on(p).start()
        rcopy(bgs, BG.at[4], bg_s.at[2], bg_r.at[4], hub).wait_recv()
        rcopy(BG.at[4], BG.at[4], bg_s.at[2], bg_r.at[4], hub_dst).start()
        pl.semaphore_wait(go, 1)
        begin(e3_dst, 1)
        sent(e3_dst, 1)
        sent(f2_dst, 0)
        for p in range(4):
            hub_on(p).wait_send()
        rcopy(BG.at[4], BG.at[4], bg_s.at[2], bg_r.at[4], hub_dst).wait_send()
        told((f2_dst, e3_dst))

    @pl.when(cross1)
    def _():
        tell((e1_dst,))
        begin(e1_dst, 0)
        sent(e1_dst, 0)
        told((e1_dst,))

    @pl.when(cross2)
    def _():
        for_hub = rcopy(bgs, BG.at[4], bg_s.at[1], bg_r.at[4], hub)
        for_hub.start()
        tell((e2_dst,))
        for p in range(4):
            hub_in(p).start()

        @pl.when(x == 0)
        def _():
            begin(e2_dst, 0)
        for p in range(4):
            hub_in(p).wait_send()

        @pl.when(x != 0)
        def _():
            begin(e2_dst, 0)
        sent(e2_dst, 0)
        told((e2_dst,))
        for_hub.wait_send()

    @pl.when(active)
    def _():
        tell(f1_dst)
        for n, d in enumerate(f1_dst):
            begin(d, n)
        own_w = pltpu.make_async_copy(weight, W.at[0], loc.at[0])
        own_w.start()
        BG[0] = bgs[...]

        def tile_of(i):
            pos = i // 2
            if isinstance(i, int):
                rel = (2, 1, 3, 0)[pos]
            else:
                rel = jnp.where(pos == 0, 2, jnp.where(pos == 1, 1, jnp.where(pos == 2, 3, 0)))
            return c * 8 + 2 * lax.rem(y + rel, 4) + (i % 2 if isinstance(i, int) else lax.rem(i, 2))

        @pl.loop(0, 8)
        def _(i):
            g = tile_of(i)
            row = lax.broadcasted_iota(jnp.int32, (16, 128), 0)
            col = lax.broadcasted_iota(jnp.int32, (16, 128), 1)
            for side in range(4):
                flip = nb[2, side, g]
                want = side * 16 + row + flip * (15 - 2 * row)
                PM[i, side * 16:side * 16 + 16, :] = jnp.where(col == want, 1.0, 0.0).astype(BF16)
            want = jnp.zeros((16, 128), jnp.int32) - 1
            for corner in range(4):
                which = nb[1, 4 + corner, g]
                last = 15 * (((which + 1) >> 1) & 1)
                want = jnp.where(row == corner, 64 + corner * 16 + last, want)
            PM[i, 64:80, :] = jnp.where(col == want, 1.0, 0.0).astype(BF16)

        @pl.loop(0, 8)
        def _(i):
            rcopy(metric.at[0], metr.at[i], met_s.at[0], met_r.at[i], partner).wait_recv()
            for q in range(9):
                line = jnp.broadcast_to(0.5 * metr[i, q:q + 1, :].astype(F32), (128, C))
                MB[i, q] = line.T.astype(BF16)

        def normed(values, k):
            mean_sq = jnp.mean(values * values, axis=-1, keepdims=True)
            return (values * lax.rsqrt(mean_sq + 1e-05) * BG[k, 8:9, :].astype(F32)).astype(BF16)

        def keep_rim(i, rim, z):
            g = tile_of(i)
            cube = z.astype(F32).reshape(16, 16, C)
            rim[4 * g] = z[0:16]
            rim[4 * g + 1] = cube[:, 15, :].astype(BF16)
            rim[4 * g + 2] = z[240:256]
            rim[4 * g + 3] = cube[:, 0, :].astype(BF16)

        def rim_copy(p, rim, par, who):
            own = pl.ds(4 * (tile_of(2 * p) + 8 * (who - c)), 8)
            return rcopy(rim.at[own], rim.at[own], rim_s.at[par, p], rim_r.at[par, p], partner)

        @pl.loop(0, 4)
        def _(p):
            for i in (2 * p, 2 * p + 1):
                rcopy(act.at[0], V.at[i], act_s.at[0], act_r.at[i], partner).wait_recv()
                z = normed(V[i].astype(F32), 0)
                Z[i] = z
                keep_rim(i, rim_a, z)
            rim_copy(p, rim_a, 0, c).start()

        pl.semaphore_signal(go, inc=1, device_id=e3_src, device_id_type=MESH)
        own_w.wait()
        for k in range(1, 8):
            rcopy(bgs, BG.at[k], bg_s.at[0], bg_r.at[k], partner).wait_recv()

        def exchange(k):
            return rcopy(W.at[k, mine], W.at[k, mine], x_s.at[k], x_r.at[k], partner)

        other = pl.ds(pl.multiple_of((1 - c) * HALF, HALF), HALF)

        def out_copy(i):
            g = tile_of(i)
            micro = y // 2
            return rcopy(V.at[i], out.at[micro], out_s.at[i], out_r.at[micro], (s, g))

        def own_copy(i):
            micro = y // 2
            return pltpu.make_async_copy(V.at[i], out.at[micro], out_r.at[micro])

        def tile_step(i, k, rim_in, rim_out):
            g = tile_of(i)
            pieces = []
            for side in range(4):
                pieces.append(rim_in[4 * nb[0, side, g] + nb[1, side, g]])
            for corner in range(4, 8):
                pieces.append(rim_in[4 * nb[0, corner, g] + (nb[1, corner, g] & 2)])
            frame = jnp.dot(PM[i], jnp.concatenate(pieces, axis=0), preferred_element_type=F32)
            z = Z[i].astype(F32)
            for h in range(2):
                lanes = slice(h * 128, h * 128 + 128)
                f, zh = frame[:, lanes], z[:, lanes]
                pad[i % 2, h, 1:17, :] = f[0:16]
                pad[i % 2, h, pl.ds(PITCH + 17, 16, stride=PITCH), :] = f[16:32]
                pad[i % 2, h, 17 * PITCH + 1:17 * PITCH + 17, :] = f[32:48]
                pad[i % 2, h, pl.ds(PITCH, 16, stride=PITCH), :] = f[48:64]
                pad[i % 2, h, 0:1, :] = f[64:65]
                pad[i % 2, h, 17:18, :] = f[65:66]
                pad[i % 2, h, 17 * PITCH + 17:17 * PITCH + 18, :] = f[66:67]
                pad[i % 2, h, 17 * PITCH:17 * PITCH + 1, :] = f[67:68]
                for r in range(16):
                    pad[i % 2, h, (r + 1) * PITCH + 1:(r + 1) * PITCH + 17, :] = zh[r * 16:r * 16 + 16]
            total = None
            for b in range(3):
                shifted = [
                    jnp.concatenate(
                        [pad[i % 2, h, r * PITCH + b:r * PITCH + b + 16, :].astype(BF16) for r in range(18)], axis=0
                    )
                    for h in range(2)
                ]
                for a in range(3):
                    q = 3 * a + b
                    lhs = jnp.concatenate([sh[a * 16:a * 16 + 256] * MB[i, q] for sh in shifted], axis=1)
                    part = jnp.dot(lhs, W[k, q * C:q * C + C, :], preferred_element_type=F32)
                    total = part if total is None else total + part
            half = total + 0.5 * BG[k, 0:1, :].astype(F32)
            v = (V[i].astype(F32) + half + half * jnp.tanh(half)).astype(BF16)
            V[i] = v

            nz = normed(v.astype(F32), lax.rem(k + 1, 8))
            Z[i] = nz
            keep_rim(i, rim_out, nz)

        def deliver(i):
            g = tile_of(i)

            @pl.when(t == g)
            def _():
                own_copy(i).start()

            @pl.when(t != g)
            def _():
                out_copy(i).start()

        def layer(k, rim_in, par_in, rim_out, par_out):
            for p in range(4):
                rim_copy(p, rim_in, par_in, 1 - c).wait_recv()

            @pl.when(k > 0)
            def _():
                rcopy(W.at[k, other], W.at[k, other], x_s.at[k], x_r.at[k], partner).wait_recv()

            for p in range(4):
                for i in (2 * p, 2 * p + 1):
                    tile_step(i, k, rim_in, rim_out)
                rim_copy(p, rim_out, par_out, c).start()
                if p == 1:
                    @pl.when(k < 7)
                    def _():
                        arrived(k + 1)
                        exchange(k + 1).start()
                if p % 2 == 1 and par_out == 0:
                    @pl.when(k == 7)
                    def _():
                        for i in range(2 * p - 2, 2 * p + 2):
                            deliver(i)

        @pl.loop(0, 4)
        def _(n):
            @pl.when(n > 0)
            def _():
                for p in range(4):
                    rim_copy(p, rim_b, 1, c).wait_send()
            layer(2 * n, rim_a, 0, rim_b, 1)
            for p in range(4):
                rim_copy(p, rim_a, 0, c).wait_send()
            layer(2 * n + 1, rim_b, 1, rim_a, 0)

        for p in range(4):
            rim_copy(p, rim_b, 1, c).wait_send()
            rim_copy(p, rim_a, 0, c).wait_send()
            rim_copy(p, rim_a, 0, 1 - c).wait_recv()
        for k in range(1, 8):
            exchange(k).wait_send()
        for n, d in enumerate(f1_dst):
            sent(d, n)
        told(f1_dst)
        for i in range(8):
            @pl.when(t != tile_of(i))
            def _():
                out_copy(i).wait_send()

    for j in range(2):
        @pl.when(jnp.logical_not(is_home[j]))
        def _():
            rcopy(metric.at[0], metr.at[slots[j]], met_s.at[j], met_r.at[slots[j]], homes[j]).wait_send()
            rcopy(act.at[j], V.at[slots[j]], act_s.at[j], act_r.at[slots[j]], homes[j]).wait_send()
        rcopy(V.at[0], out.at[j], out_s.at[0], out_r.at[j], partner).wait_recv()


def local(activations, weight, conv_bias, norm_gain, metric, neighbours):
    anywhere = pl.BlockSpec(memory_space=pl.ANY)
    vmem = pl.BlockSpec(memory_space=pltpu.VMEM)
    dma = pltpu.SemaphoreType.DMA
    out = pl.pallas_call(
        kernel,
        name="sphere",
        out_shape=jax.ShapeDtypeStruct((2, C, C), BF16),
        in_specs=[pl.BlockSpec(memory_space=pltpu.SMEM), anywhere, anywhere, anywhere, vmem, vmem],
        out_specs=anywhere,
        scratch_shapes=[
            pltpu.VMEM((8, 9 * C, C), BF16),
            pltpu.VMEM((8, C, C), BF16),
            pltpu.VMEM((8, C, C), BF16),
            pltpu.VMEM((64, 16, C), BF16),
            pltpu.VMEM((64, 16, C), BF16),
            pltpu.VMEM((8, 9, C), BF16),
            pltpu.VMEM((8, 9, C, 128), BF16),
            pltpu.VMEM((8, 16, C), BF16),
            pltpu.VMEM((16, C), BF16),
            pltpu.VMEM((8, 80, 128), BF16),
            pltpu.VMEM((2, 2, 336, 128), F32),
            dma((2,)), dma((8,)), dma((2,)), dma((8,)),
            dma((3,)), dma((8,)), dma((3,)), dma((8,)),
            dma((8,)), dma((8,)),
            dma((2, 4)), dma((2, 4)), dma((8,)), dma((2,)), dma((1,)), dma((4,)), dma((4,)),
            pltpu.SemaphoreType.REGULAR,
        ],
        compiler_params=pltpu.CompilerParams(
            collective_id=0, has_side_effects=True
        ),
    )(
        neighbours.transpose(0, 2, 1),
        activations.reshape(2, C, C),
        weight.reshape(9 * C, C),
        metric,
        conv_bias,
        norm_gain,
    )
    return out.reshape(2, 1, 16, 16, C)


def solution(mesh):
    in_specs = (
        P("section", "tile", None, None, None),
        P("section", None, None, None),
        P("section", None),
        P("section", None),
        P("tile", None, None),
        P(),
    )
    out_specs = P("section", "tile", None, None, None)
    return jax.shard_map(local, mesh=mesh, in_specs=in_specs, out_specs=out_specs, check_vma=False)
```

```python
import jax
import jax.numpy as jnp
from jax import lax
from jax.experimental import pallas as pl
from jax.experimental.pallas import tpu as pltpu
from jax.sharding import PartitionSpec as P

MESH = pl.DeviceIdType.MESH
C = 256
HALF = 9 * C // 2
F32, BF16 = jnp.float32, jnp.bfloat16
PITCH = 18


def rcopy(src, dst, send, recv, device):
    return pltpu.make_async_remote_copy(
        src_ref=src, dst_ref=dst, send_sem=send, recv_sem=recv, device_id=device, device_id_type=MESH
    )


def kernel(
    nb, act, weight, metric, bias, gain, out,
    W, V, Z, rim_a, rim_b, metr, MB, BG, bgs, PM, pad,
    act_s, act_r, met_s, met_r, w_s, w_r, bg_s, bg_r, x_s, x_r,
    rim_s, rim_r, out_s, out_r, loc, hub_s, hub_r, go,
):
    s, t = lax.axis_index("section"), lax.axis_index("tile")
    hi, x = s // 4, lax.rem(s, 4)
    zl, y, c = t // 8, lax.rem(t // 2, 4), lax.rem(t, 2)
    even = lax.rem(y, 2) == 0
    active = jnp.logical_and(zl == 1, even)
    relay = jnp.logical_and(zl == 1, jnp.logical_not(even))
    cross1 = jnp.logical_and(zl == 0, even)
    cross2 = jnp.logical_and(zl == 0, jnp.logical_not(even))

    def sec(h, xx):
        return h * 4 + lax.rem(xx + 8, 4)

    def tid(plane, row, core):
        return plane * 8 + 2 * lax.rem(row + 4, 4) + core

    partner = (s, t + 1 - 2 * c)
    homes = [(s, 8 + zl), (s, 12 + zl)]
    is_home = [t == 8 + zl, t == 12 + zl]

    f1_dst = [(sec(hi, x - 1), t), (sec(hi, x + 1), t)]
    f2_dst = (sec(hi, x + 2), tid(1, y - 1, c))
    e3_dst = (sec(1 - hi, x + 1), t)
    hub_dst = (s, tid(1, y + 1, c))
    hub_src = (sec(1 - hi, jnp.where(x == 3, 1, x)), tid(0, y, c))
    hub_k = jnp.where(x == 3, 2, 4)
    e3_hub = (e3_dst[0], tid(0, y, c))
    hub3_src = (sec(1 - hi, x - 1), tid(1, y, c))
    hub3_dst = (s, tid(1, y, c))
    hub3_k = lax.rem(hub3_src[0] - s + 8, 8)
    near = (sec(1 - hi, x), tid(1, jnp.where(x == 3, y + 1, y), c))
    far = (sec(1 - hi, x + 2), tid(1, jnp.where(x == 1, y, y - 1), c))
    e1_dst = (sec(1 - hi, x - 1), tid(1, y, c))
    e3_src = (sec(1 - hi, x - 1), t)
    w_src = [
        (sec(hi, x + 1), t), (sec(hi, x - 1), t), (sec(hi, x + 2), tid(1, y + 1, c)), (s, tid(1, y - 1, c)), e3_src,
        (s, tid(0, y, c)), (sec(1 - hi, x + 1), tid(0, y, c)),
        (sec(1 - hi, jnp.where(x == 3, x, x + 2)), tid(0, jnp.where(x == 3, y - 1, y + 1), c)),
    ]

    barrier = pltpu.get_barrier_semaphore()

    def hello(device):
        pl.semaphore_signal(barrier, inc=1, device_id=device, device_id_type=MESH)

    for j in range(2):
        @pl.when(jnp.logical_not(is_home[j]))
        def _():
            hello(homes[j])

    @pl.when(active)
    def _():
        for i in range(8):
            @pl.when(t != c * 8 + i)
            def _():
                hello((s, c * 8 + i))
        for d in w_src + [e3_dst, e3_hub]:
            hello(d)
        hello(partner)

    @pl.when(relay)
    def _():
        for d in (f2_dst, hub_dst, hub_src):
            hello(d)

    @pl.when(cross1)
    def _():
        for d in (e1_dst, hub3_src, hub3_dst):
            hello(d)

    @pl.when(cross2)
    def _():
        hello(near)
        hello(far)

    at_home = jnp.logical_or(is_home[0], is_home[1])
    greeted = jnp.where(at_home, 1, 2) + jnp.where(relay, 3, jnp.where(active, jnp.where(c == zl, 18, 19), 3 - lax.rem(y, 2)))
    pl.semaphore_wait(barrier, greeted)

    def place(row, row0):
        rel = lax.rem(row - row0 + 4, 4)
        return jnp.where(rel == 0, 3, jnp.where(rel == 1, 1, jnp.where(rel == 2, 0, 2)))

    slots = [2 * place(y, 2 * j) + c for j in range(2)]
    for j in range(2):
        @pl.when(is_home[j])
        def _():
            pltpu.make_async_copy(metric.at[0], metr.at[slots[j]], met_r.at[slots[j]]).start()
            pltpu.make_async_copy(act.at[j], V.at[slots[j]], act_r.at[slots[j]]).start()

        @pl.when(jnp.logical_not(is_home[j]))
        def _():
            rcopy(metric.at[0], metr.at[slots[j]], met_s.at[j], met_r.at[slots[j]], homes[j]).start()
            rcopy(act.at[j], V.at[slots[j]], act_s.at[j], act_r.at[slots[j]], homes[j]).start()

    bgs[0:8] = jnp.broadcast_to(bias[...], (8, C))
    bgs[8:16] = jnp.broadcast_to(gain[...], (8, C))

    mine = pl.ds(pl.multiple_of(c * HALF, HALF), HALF)

    def stream(device, n):
        k = lax.rem(s - device[0] + 8, 8)
        return rcopy(weight.at[mine], W.at[k, mine], w_s.at[n], w_r.at[k], device)

    def begin(device, n):
        stream(device, n).start()

    def sent(device, n):
        stream(device, n).wait_send()

    def lines(device, n):
        k = lax.rem(s - device[0] + 8, 8)
        return rcopy(bgs, BG.at[k], bg_s.at[n], bg_r.at[k], device)

    def tell(devices):
        for n, d in enumerate(devices):
            lines(d, n).start()

    def told(devices):
        for n, d in enumerate(devices):
            lines(d, n).wait_send()

    def arrived(k):
        rcopy(weight.at[mine], W.at[k, mine], w_s.at[0], w_r.at[k], partner).wait_recv()

    PART = HALF // 4

    def part(p, n=1):
        return pl.ds(pl.multiple_of(c * HALF + p * PART, 16), n * PART)

    def hub_in(p, device, n):
        k = lax.rem(s - device[0] + 8, 8)
        return rcopy(weight.at[part(p)], W.at[k, part(p)], hub_s.at[n + p], hub_r.at[p], device)

    def hub_on(p):
        return rcopy(W.at[hub_k, part(p)], W.at[hub_k, part(p)], hub_s.at[p], w_r.at[hub_k], hub_dst)

    def hub3_in(p):
        k = lax.rem(s - e3_hub[0] + 8, 8)
        return rcopy(weight.at[part(p)], W.at[k, part(p)], hub_s.at[4 + p], hub_r.at[p], e3_hub)

    def hub3_on(p):
        return rcopy(W.at[hub3_k, part(p)], W.at[hub3_k, part(p)], hub_s.at[p], w_r.at[hub3_k], hub3_dst)

    @pl.when(relay)
    def _():
        tell((f2_dst,))

        @pl.when(x >= 2)
        def _():
            begin(f2_dst, 0)
        for p in range(4):
            rcopy(weight.at[part(p)], W.at[hub_k, part(p)], hub_s.at[p], hub_r.at[p], f2_dst).wait_recv()
            hub_on(p).start()
        rcopy(bgs, BG.at[hub_k], bg_s.at[2], bg_r.at[hub_k], f2_dst).wait_recv()
        hub_line = rcopy(BG.at[hub_k], BG.at[hub_k], bg_s.at[2], bg_r.at[hub_k], hub_dst)
        hub_line.start()

        @pl.when(x < 2)
        def _():
            begin(f2_dst, 0)
        sent(f2_dst, 0)
        for p in range(4):
            hub_on(p).wait_send()
        hub_line.wait_send()
        told((f2_dst,))

    @pl.when(cross1)
    def _():
        tell((e1_dst,))

        @pl.when(x == 0)
        def _():
            begin(e1_dst, 0)
        pl.semaphore_wait(go, 1)

        @pl.when(x != 0)
        def _():
            begin(e1_dst, 0)
        for p in range(4):
            rcopy(weight.at[part(p)], W.at[hub3_k, part(p)], hub_s.at[p], hub_r.at[p], e1_dst).wait_recv()
            hub3_on(p).start()
        sent(e1_dst, 0)
        for p in range(4):
            hub3_on(p).wait_send()
        told((e1_dst,))

    def halves(n):
        k = lax.rem(s - far[0] + 8, 8)
        return rcopy(weight.at[part(2 * n, 2)], W.at[k, part(2 * n, 2)], w_s.at[2 * n], w_r.at[k], far)

    @pl.when(cross2)
    def _():
        tell((near, far))

        @pl.when(x == 3)
        def _():
            halves(0).start()
            halves(0).wait_send()
            begin(near, 1)
            sent(near, 1)
            halves(1).start()
            halves(1).wait_send()

        @pl.when(x == 1)
        def _():
            for p in range(4):
                hub_in(p, far, 4).start()

        @pl.when(x == 0)
        def _():
            begin(far, 0)

        @pl.when(x != 3)
        def _():
            for p in range(4):
                hub_in(p, near, 0).start()
            for p in range(4):
                hub_in(p, near, 0).wait_send()

        @pl.when(x == 1)
        def _():
            for p in range(4):
                hub_in(p, far, 4).wait_send()

        @pl.when(x == 2)
        def _():
            begin(far, 0)

        @pl.when(jnp.logical_or(x == 0, x == 2))
        def _():
            sent(far, 0)
        told((near, far))

    @pl.when(active)
    def _():
        tell(f1_dst + [e3_dst])
        for p in range(4):
            hub3_in(p).start()
        for n, d in enumerate(f1_dst):
            begin(d, n)
        own_w = pltpu.make_async_copy(weight, W.at[0], loc.at[0])
        own_w.start()
        BG[0] = bgs[...]

        def tile_of(i):
            pos = i // 2
            if isinstance(i, int):
                rel = (2, 1, 3, 0)[pos]
            else:
                rel = jnp.where(pos == 0, 2, jnp.where(pos == 1, 1, jnp.where(pos == 2, 3, 0)))
            return c * 8 + 2 * lax.rem(y + rel, 4) + (i % 2 if isinstance(i, int) else lax.rem(i, 2))

        @pl.loop(0, 8)
        def _(i):
            g = tile_of(i)
            row = lax.broadcasted_iota(jnp.int32, (16, 128), 0)
            col = lax.broadcasted_iota(jnp.int32, (16, 128), 1)
            for side in range(4):
                flip = nb[2, side, g]
                want = side * 16 + row + flip * (15 - 2 * row)
                PM[i, side * 16:side * 16 + 16, :] = jnp.where(col == want, 1.0, 0.0).astype(BF16)
            want = jnp.zeros((16, 128), jnp.int32) - 1
            for corner in range(4):
                which = nb[1, 4 + corner, g]
                last = 15 * (((which + 1) >> 1) & 1)
                want = jnp.where(row == corner, 64 + corner * 16 + last, want)
            PM[i, 64:80, :] = jnp.where(col == want, 1.0, 0.0).astype(BF16)

        @pl.loop(0, 8)
        def _(i):
            rcopy(metric.at[0], metr.at[i], met_s.at[0], met_r.at[i], partner).wait_recv()
            for q in range(9):
                line = jnp.broadcast_to(0.5 * metr[i, q:q + 1, :].astype(F32), (128, C))
                MB[i, q] = line.T.astype(BF16)

        def normed(values, k):
            mean_sq = jnp.mean(values * values, axis=-1, keepdims=True)
            return (values * lax.rsqrt(mean_sq + 1e-05) * BG[k, 8:9, :].astype(F32)).astype(BF16)

        def keep_rim(i, rim, z):
            g = tile_of(i)
            cube = z.astype(F32).reshape(16, 16, C)
            rim[4 * g] = z[0:16]
            rim[4 * g + 1] = cube[:, 15, :].astype(BF16)
            rim[4 * g + 2] = z[240:256]
            rim[4 * g + 3] = cube[:, 0, :].astype(BF16)

        def rim_copy(p, rim, par, who):
            own = pl.ds(4 * (tile_of(2 * p) + 8 * (who - c)), 8)
            return rcopy(rim.at[own], rim.at[own], rim_s.at[par, p], rim_r.at[par, p], partner)

        @pl.loop(0, 4)
        def _(p):
            for i in (2 * p, 2 * p + 1):
                rcopy(act.at[0], V.at[i], act_s.at[0], act_r.at[i], partner).wait_recv()
                z = normed(V[i].astype(F32), 0)
                Z[i] = z
                keep_rim(i, rim_a, z)
            rim_copy(p, rim_a, 0, c).start()

        own_w.wait()
        for k in range(1, 8):
            rcopy(bgs, BG.at[k], bg_s.at[0], bg_r.at[k], partner).wait_recv()

        def exchange(k):
            return rcopy(W.at[k, mine], W.at[k, mine], x_s.at[k], x_r.at[k], partner)

        other = pl.ds(pl.multiple_of((1 - c) * HALF, HALF), HALF)

        def out_copy(i):
            g = tile_of(i)
            micro = y // 2
            return rcopy(V.at[i], out.at[micro], out_s.at[i], out_r.at[micro], (s, g))

        def own_copy(i):
            micro = y // 2
            return pltpu.make_async_copy(V.at[i], out.at[micro], out_r.at[micro])

        def tile_step(i, k, rim_in, rim_out):
            g = tile_of(i)
            pieces = []
            for side in range(4):
                pieces.append(rim_in[4 * nb[0, side, g] + nb[1, side, g]])
            for corner in range(4, 8):
                pieces.append(rim_in[4 * nb[0, corner, g] + (nb[1, corner, g] & 2)])
            frame = jnp.dot(PM[i], jnp.concatenate(pieces, axis=0), preferred_element_type=F32)
            z = Z[i].astype(F32)
            for h in range(2):
                lanes = slice(h * 128, h * 128 + 128)
                f, zh = frame[:, lanes], z[:, lanes]
                pad[i % 2, h, 1:17, :] = f[0:16]
                pad[i % 2, h, pl.ds(PITCH + 17, 16, stride=PITCH), :] = f[16:32]
                pad[i % 2, h, 17 * PITCH + 1:17 * PITCH + 17, :] = f[32:48]
                pad[i % 2, h, pl.ds(PITCH, 16, stride=PITCH), :] = f[48:64]
                pad[i % 2, h, 0:1, :] = f[64:65]
                pad[i % 2, h, 17:18, :] = f[65:66]
                pad[i % 2, h, 17 * PITCH + 17:17 * PITCH + 18, :] = f[66:67]
                pad[i % 2, h, 17 * PITCH:17 * PITCH + 1, :] = f[67:68]
                for r in range(16):
                    pad[i % 2, h, (r + 1) * PITCH + 1:(r + 1) * PITCH + 17, :] = zh[r * 16:r * 16 + 16]
            total = None
            for b in range(3):
                shifted = [
                    jnp.concatenate(
                        [pad[i % 2, h, r * PITCH + b:r * PITCH + b + 16, :].astype(BF16) for r in range(18)], axis=0
                    )
                    for h in range(2)
                ]
                for a in range(3):
                    q = 3 * a + b
                    lhs = jnp.concatenate([sh[a * 16:a * 16 + 256] * MB[i, q] for sh in shifted], axis=1)
                    part = jnp.dot(lhs, W[k, q * C:q * C + C, :], preferred_element_type=F32)
                    total = part if total is None else total + part
            half = total + 0.5 * BG[k, 0:1, :].astype(F32)
            v = (V[i].astype(F32) + half + half * jnp.tanh(half)).astype(BF16)
            V[i] = v

            nz = normed(v.astype(F32), lax.rem(k + 1, 8))
            Z[i] = nz
            keep_rim(i, rim_out, nz)

        def deliver(i):
            g = tile_of(i)

            @pl.when(t == g)
            def _():
                own_copy(i).start()

            @pl.when(t != g)
            def _():
                out_copy(i).start()

        def layer(k, rim_in, par_in, rim_out, par_out):
            for p in range(4):
                rim_copy(p, rim_in, par_in, 1 - c).wait_recv()
            if par_in == 0:
                @pl.when(k == 0)
                def _():
                    pl.semaphore_signal(go, inc=1, device_id=(s, tid(0, y, c)), device_id_type=MESH)

            @pl.when(k > 0)
            def _():
                rcopy(W.at[k, other], W.at[k, other], x_s.at[k], x_r.at[k], partner).wait_recv()

            for p in range(4):
                for i in (2 * p, 2 * p + 1):
                    tile_step(i, k, rim_in, rim_out)
                rim_copy(p, rim_out, par_out, c).start()
                if p == 1:
                    @pl.when(k < 7)
                    def _():
                        arrived(k + 1)
                        exchange(k + 1).start()
                if p % 2 == 1 and par_out == 0:
                    @pl.when(k == 7)
                    def _():
                        for i in range(2 * p - 2, 2 * p + 2):
                            deliver(i)

        @pl.loop(0, 4)
        def _(n):
            @pl.when(n > 0)
            def _():
                for p in range(4):
                    rim_copy(p, rim_b, 1, c).wait_send()
            layer(2 * n, rim_a, 0, rim_b, 1)
            for p in range(4):
                rim_copy(p, rim_a, 0, c).wait_send()
            layer(2 * n + 1, rim_b, 1, rim_a, 0)

        for p in range(4):
            rim_copy(p, rim_b, 1, c).wait_send()
            rim_copy(p, rim_a, 0, c).wait_send()
            rim_copy(p, rim_a, 0, 1 - c).wait_recv()
        for k in range(1, 8):
            exchange(k).wait_send()
        for n, d in enumerate(f1_dst):
            sent(d, n)
        for p in range(4):
            hub3_in(p).wait_send()
        told(f1_dst + [e3_dst])
        for i in range(8):
            @pl.when(t != tile_of(i))
            def _():
                out_copy(i).wait_send()

    for j in range(2):
        @pl.when(jnp.logical_not(is_home[j]))
        def _():
            rcopy(metric.at[0], metr.at[slots[j]], met_s.at[j], met_r.at[slots[j]], homes[j]).wait_send()
            rcopy(act.at[j], V.at[slots[j]], act_s.at[j], act_r.at[slots[j]], homes[j]).wait_send()
        rcopy(V.at[0], out.at[j], out_s.at[0], out_r.at[j], partner).wait_recv()


def local(activations, weight, conv_bias, norm_gain, metric, neighbours):
    anywhere = pl.BlockSpec(memory_space=pl.ANY)
    vmem = pl.BlockSpec(memory_space=pltpu.VMEM)
    dma = pltpu.SemaphoreType.DMA
    out = pl.pallas_call(
        kernel,
        name="sphere",
        out_shape=jax.ShapeDtypeStruct((2, C, C), BF16),
        in_specs=[pl.BlockSpec(memory_space=pltpu.SMEM), anywhere, anywhere, anywhere, vmem, vmem],
        out_specs=anywhere,
        scratch_shapes=[
            pltpu.VMEM((8, 9 * C, C), BF16),
            pltpu.VMEM((8, C, C), BF16),
            pltpu.VMEM((8, C, C), BF16),
            pltpu.VMEM((64, 16, C), BF16),
            pltpu.VMEM((64, 16, C), BF16),
            pltpu.VMEM((8, 9, C), BF16),
            pltpu.VMEM((8, 9, C, 128), BF16),
            pltpu.VMEM((8, 16, C), BF16),
            pltpu.VMEM((16, C), BF16),
            pltpu.VMEM((8, 80, 128), BF16),
            pltpu.VMEM((2, 2, 336, 128), F32),
            dma((2,)), dma((8,)), dma((2,)), dma((8,)),
            dma((3,)), dma((8,)), dma((3,)), dma((8,)),
            dma((8,)), dma((8,)),
            dma((2, 4)), dma((2, 4)), dma((8,)), dma((2,)), dma((1,)), dma((8,)), dma((4,)),
            pltpu.SemaphoreType.REGULAR,
        ],
        compiler_params=pltpu.CompilerParams(
            collective_id=0, has_side_effects=True
        ),
    )(
        neighbours.transpose(0, 2, 1),
        activations.reshape(2, C, C),
        weight.reshape(9 * C, C),
        metric,
        conv_bias,
        norm_gain,
    )
    return out.reshape(2, 1, 16, 16, C)


def solution(mesh):
    in_specs = (
        P("section", "tile", None, None, None),
        P("section", None, None, None),
        P("section", None),
        P("section", None),
        P("tile", None, None),
        P(),
    )
    out_specs = P("section", "tile", None, None, None)
    return jax.shard_map(local, mesh=mesh, in_specs=in_specs, out_specs=out_specs, check_vma=False)
```

```python
import jax
import jax.numpy as jnp
from jax import lax
from jax.experimental import pallas as pl
from jax.experimental.pallas import tpu as pltpu
from jax.sharding import PartitionSpec as P

MESH = pl.DeviceIdType.MESH
C = 256
HALF = 9 * C // 2
F32, BF16 = jnp.float32, jnp.bfloat16
PITCH = 18


def rcopy(src, dst, send, recv, device):
    return pltpu.make_async_remote_copy(
        src_ref=src, dst_ref=dst, send_sem=send, recv_sem=recv, device_id=device, device_id_type=MESH
    )


def kernel(
    nb, act, weight, metric, bias, gain, out,
    W, V, Z, rim_a, rim_b, metr, MB, BG, bgs, PM, pad,
    act_s, act_r, met_s, met_r, w_s, w_r, bg_s, bg_r, x_s, x_r,
    rim_s, rim_r, out_s, out_r, loc, hub_s, hub_r, go,
    bare, early, PMC, MBC,
):
    s, t = lax.axis_index("section"), lax.axis_index("tile")
    hi, x = s // 4, lax.rem(s, 4)
    zl, y, c = t // 8, lax.rem(t // 2, 4), lax.rem(t, 2)
    even = lax.rem(y, 2) == 0
    active = jnp.logical_and(zl == 1, even)
    relay = jnp.logical_and(zl == 1, jnp.logical_not(even))
    cross1 = jnp.logical_and(zl == 0, even)
    cross2 = jnp.logical_and(zl == 0, jnp.logical_not(even))

    def sec(h, xx):
        return h * 4 + lax.rem(xx + 8, 4)

    def tid(plane, row, core):
        return plane * 8 + 2 * lax.rem(row + 4, 4) + core

    partner = (s, t + 1 - 2 * c)
    homes = [(s, 8 + zl), (s, 12 + zl)]
    is_home = [t == 8 + zl, t == 12 + zl]

    f1_dst = [(sec(hi, x - 1), t), (sec(hi, x + 1), t)]
    f2_dst = (sec(hi, x + 2), tid(1, y - 1, c))
    e3_dst = (sec(1 - hi, x + 1), t)
    hub_dst = (s, tid(1, y + 1, c))
    hub_src = (sec(1 - hi, jnp.where(x == 3, 1, x)), tid(0, y, c))
    hub_k = jnp.where(x == 3, 2, 4)
    e3_hub = (e3_dst[0], tid(0, y, c))
    hub3_src = (sec(1 - hi, x - 1), tid(1, y, c))
    hub3_dst = (s, tid(1, y, c))
    hub3_k = lax.rem(hub3_src[0] - s + 8, 8)
    near = (sec(1 - hi, x), tid(1, jnp.where(x == 3, y + 1, y), c))
    far = (sec(1 - hi, x + 2), tid(1, jnp.where(x == 1, y, y - 1), c))
    e1_dst = (sec(1 - hi, x - 1), tid(1, y, c))
    e3_src = (sec(1 - hi, x - 1), t)
    w_src = [
        (sec(hi, x + 1), t), (sec(hi, x - 1), t), (sec(hi, x + 2), tid(1, y + 1, c)), (s, tid(1, y - 1, c)), e3_src,
        (s, tid(0, y, c)), (sec(1 - hi, x + 1), tid(0, y, c)),
        (sec(1 - hi, jnp.where(x == 3, x, x + 2)), tid(0, jnp.where(x == 3, y - 1, y + 1), c)),
    ]

    barrier = pltpu.get_barrier_semaphore()

    def hello(device):
        pl.semaphore_signal(barrier, inc=1, device_id=device, device_id_type=MESH)

    for j in range(2):
        @pl.when(jnp.logical_not(is_home[j]))
        def _():
            hello(homes[j])

    @pl.when(active)
    def _():
        for i in range(8):
            @pl.when(t != c * 8 + i)
            def _():
                hello((s, c * 8 + i))
        for d in w_src + [e3_dst, e3_hub]:
            hello(d)
        hello(partner)

    @pl.when(relay)
    def _():
        for d in (f2_dst, hub_dst, hub_src):
            hello(d)

    @pl.when(cross1)
    def _():
        for d in (e1_dst, hub3_src, hub3_dst):
            hello(d)

    @pl.when(cross2)
    def _():
        hello(near)
        hello(far)

    at_home = jnp.logical_or(is_home[0], is_home[1])
    greeted = jnp.where(at_home, 1, 2) + jnp.where(relay, 3, jnp.where(active, jnp.where(c == zl, 18, 19), 3 - lax.rem(y, 2)))
    pl.semaphore_wait(barrier, greeted)

    def place(row, row0):
        rel = lax.rem(row - row0 + 4, 4)
        return jnp.where(rel == 0, 3, jnp.where(rel == 1, 1, jnp.where(rel == 2, 0, 2)))

    slots = [2 * place(y, 2 * j) + c for j in range(2)]
    for j in range(2):
        @pl.when(is_home[j])
        def _():
            pltpu.make_async_copy(metric.at[0], metr.at[slots[j]], met_r.at[slots[j]]).start()
            pltpu.make_async_copy(act.at[j], V.at[slots[j]], act_r.at[slots[j]]).start()

        @pl.when(jnp.logical_not(is_home[j]))
        def _():
            rcopy(metric.at[0], metr.at[slots[j]], met_s.at[j], met_r.at[slots[j]], homes[j]).start()
            rcopy(act.at[j], V.at[slots[j]], act_s.at[j], act_r.at[slots[j]], homes[j]).start()

    bgs[0:8] = jnp.broadcast_to(bias[...], (8, C))
    bgs[8:16] = jnp.broadcast_to(gain[...], (8, C))

    mine = pl.ds(pl.multiple_of(c * HALF, HALF), HALF)

    def stream(device, n):
        k = lax.rem(s - device[0] + 8, 8)
        return rcopy(weight.at[mine], W.at[k, mine], w_s.at[n], w_r.at[k], device)

    def begin(device, n):
        stream(device, n).start()

    def sent(device, n):
        stream(device, n).wait_send()

    def lines(device, n):
        k = lax.rem(s - device[0] + 8, 8)
        return rcopy(bgs, BG.at[k], bg_s.at[n], bg_r.at[k], device)

    def tell(devices):
        for n, d in enumerate(devices):
            lines(d, n).start()

    def told(devices):
        for n, d in enumerate(devices):
            lines(d, n).wait_send()

    def arrived(k):
        rcopy(weight.at[mine], W.at[k, mine], w_s.at[0], w_r.at[k], partner).wait_recv()

    PART = HALF // 4

    def part(p, n=1):
        return pl.ds(pl.multiple_of(c * HALF + p * PART, 16), n * PART)

    def hub_in(p, device, n):
        k = lax.rem(s - device[0] + 8, 8)
        return rcopy(weight.at[part(p)], W.at[k, part(p)], hub_s.at[n + p], hub_r.at[p], device)

    def hub_on(p):
        return rcopy(W.at[hub_k, part(p)], W.at[hub_k, part(p)], hub_s.at[p], w_r.at[hub_k], hub_dst)

    def hub3_in(p):
        k = lax.rem(s - e3_hub[0] + 8, 8)
        return rcopy(weight.at[part(p)], W.at[k, part(p)], hub_s.at[4 + p], hub_r.at[p], e3_hub)

    def hub3_on(p):
        return rcopy(W.at[hub3_k, part(p)], W.at[hub3_k, part(p)], hub_s.at[p], w_r.at[hub3_k], hub3_dst)

    @pl.when(relay)
    def _():
        tell((f2_dst,))

        @pl.when(x >= 2)
        def _():
            begin(f2_dst, 0)
        for p in range(4):
            rcopy(weight.at[part(p)], W.at[hub_k, part(p)], hub_s.at[p], hub_r.at[p], f2_dst).wait_recv()
            hub_on(p).start()
        rcopy(bgs, BG.at[hub_k], bg_s.at[2], bg_r.at[hub_k], f2_dst).wait_recv()
        hub_line = rcopy(BG.at[hub_k], BG.at[hub_k], bg_s.at[2], bg_r.at[hub_k], hub_dst)
        hub_line.start()

        @pl.when(x < 2)
        def _():
            begin(f2_dst, 0)
        sent(f2_dst, 0)
        for p in range(4):
            hub_on(p).wait_send()
        hub_line.wait_send()
        told((f2_dst,))

    @pl.when(cross1)
    def _():
        tell((e1_dst,))

        @pl.when(x == 0)
        def _():
            begin(e1_dst, 0)
        pl.semaphore_wait(go, 1)

        @pl.when(x != 0)
        def _():
            begin(e1_dst, 0)
        for p in range(4):
            rcopy(weight.at[part(p)], W.at[hub3_k, part(p)], hub_s.at[p], hub_r.at[p], e1_dst).wait_recv()
            hub3_on(p).start()
        sent(e1_dst, 0)
        for p in range(4):
            hub3_on(p).wait_send()
        told((e1_dst,))

    def halves(n):
        k = lax.rem(s - far[0] + 8, 8)
        return rcopy(weight.at[part(2 * n, 2)], W.at[k, part(2 * n, 2)], w_s.at[2 * n], w_r.at[k], far)

    @pl.when(cross2)
    def _():
        tell((near, far))

        @pl.when(x == 3)
        def _():
            halves(0).start()
            halves(0).wait_send()
            begin(near, 1)
            sent(near, 1)
            halves(1).start()
            halves(1).wait_send()

        @pl.when(x == 1)
        def _():
            for p in range(4):
                hub_in(p, far, 4).start()

        @pl.when(x == 0)
        def _():
            begin(far, 0)

        @pl.when(x != 3)
        def _():
            for p in range(4):
                hub_in(p, near, 0).start()
            for p in range(4):
                hub_in(p, near, 0).wait_send()

        @pl.when(x == 1)
        def _():
            for p in range(4):
                hub_in(p, far, 4).wait_send()

        @pl.when(x == 2)
        def _():
            begin(far, 0)

        @pl.when(jnp.logical_or(x == 0, x == 2))
        def _():
            sent(far, 0)
        told((near, far))

    @pl.when(active)
    def _():
        tell(f1_dst + [e3_dst])
        for p in range(4):
            hub3_in(p).start()
        for n, d in enumerate(f1_dst):
            begin(d, n)
        own_w = pltpu.make_async_copy(weight, W.at[0], loc.at[0])
        own_w.start()
        BG[0] = bgs[...]

        def tile_of(i):
            pos = i // 2
            if isinstance(i, int):
                rel = (2, 1, 3, 0)[pos]
            else:
                rel = jnp.where(pos == 0, 2, jnp.where(pos == 1, 1, jnp.where(pos == 2, 3, 0)))
            return c * 8 + 2 * lax.rem(y + rel, 4) + (i % 2 if isinstance(i, int) else lax.rem(i, 2))

        @pl.loop(0, 8)
        def _(i):
            g = tile_of(i)
            row = lax.broadcasted_iota(jnp.int32, (16, 128), 0)
            col = lax.broadcasted_iota(jnp.int32, (16, 128), 1)
            for side in range(4):
                flip = nb[2, side, g]
                want = side * 16 + row + flip * (15 - 2 * row)
                PM[i, side * 16:side * 16 + 16, :] = jnp.where(col == want, 1.0, 0.0).astype(BF16)
            want = jnp.zeros((16, 128), jnp.int32) - 1
            for corner in range(4):
                which = nb[1, 4 + corner, g]
                last = 15 * (((which + 1) >> 1) & 1)
                want = jnp.where(row == corner, 64 + corner * 16 + last, want)
            PM[i, 64:80, :] = jnp.where(col == want, 1.0, 0.0).astype(BF16)

        @pl.loop(0, 8)
        def _(i):
            rcopy(metric.at[0], metr.at[i], met_s.at[0], met_r.at[i], partner).wait_recv()
            for q in range(9):
                line = jnp.broadcast_to(0.5 * metr[i, q:q + 1, :].astype(F32), (128, C))
                MB[i, q] = line.T.astype(BF16)

        bare[...] = jnp.zeros_like(bare)
        BLOCKS = [
            (0, 0, -1, 0), (0, 1, 0, None), (0, 2, 1, 1), (2, 6, -1, 3), (2, 7, 0, None), (2, 8, 1, 2),
            (3, 0, -1, None), (3, 3, 0, None), (3, 6, 1, None), (1, 2, -1, None), (1, 5, 0, None), (1, 8, 1, None),
        ]
        for i in range(2):
            g = tile_of(i)
            row = lax.broadcasted_iota(jnp.int32, (16, 128), 0)
            col = lax.broadcasted_iota(jnp.int32, (16, 128), 1)
            for n, (side, q, shift, corner) in enumerate(BLOCKS):
                m = row + shift
                flip = nb[2, side, g]
                want = side * 16 + m + flip * (15 - 2 * m)
                beyond = -1
                if corner is not None:
                    which = nb[1, 4 + corner, g]
                    beyond = 64 + corner * 16 + 15 * (((which + 1) >> 1) & 1)
                want = jnp.where(jnp.logical_or(m < 0, m > 15), beyond, want)
                here = slice(n * 16, n * 16 + 16)
                PMC[i, here, :] = jnp.where(col == want, 1.0, 0.0).astype(BF16)
                cube = MB[i, q].astype(F32).reshape(16, 16, 128)
                edge = (cube[0], cube[:, 15], cube[15], cube[:, 0])[side]
                MBC[i, here, :] = edge.astype(BF16)

        def normed(values, k):
            mean_sq = jnp.mean(values * values, axis=-1, keepdims=True)
            return (values * lax.rsqrt(mean_sq + 1e-05) * BG[k, 8:9, :].astype(F32)).astype(BF16)

        def keep_rim(i, rim, z):
            g = tile_of(i)
            cube = z.astype(F32).reshape(16, 16, C)
            rim[4 * g] = z[0:16]
            rim[4 * g + 1] = cube[:, 15, :].astype(BF16)
            rim[4 * g + 2] = z[240:256]
            rim[4 * g + 3] = cube[:, 0, :].astype(BF16)

        def rim_copy(p, rim, par, who):
            own = pl.ds(4 * (tile_of(2 * p) + 8 * (who - c)), 8)
            return rcopy(rim.at[own], rim.at[own], rim_s.at[par, p], rim_r.at[par, p], partner)

        @pl.loop(0, 4)
        def _(p):
            for i in (2 * p, 2 * p + 1):
                rcopy(act.at[0], V.at[i], act_s.at[0], act_r.at[i], partner).wait_recv()
                z = normed(V[i].astype(F32), 0)
                Z[i] = z
                keep_rim(i, rim_a, z)
            rim_copy(p, rim_a, 0, c).start()

            @pl.when(jnp.logical_and(p == 3, c == 0))
            def _():
                for core in range(2):
                    pl.semaphore_signal(go, inc=1, device_id=(s, tid(0, y, core)), device_id_type=MESH)

        own_w.wait()
        for k in range(1, 8):
            rcopy(bgs, BG.at[k], bg_s.at[0], bg_r.at[k], partner).wait_recv()

        def exchange(k):
            return rcopy(W.at[k, mine], W.at[k, mine], x_s.at[k], x_r.at[k], partner)

        other = pl.ds(pl.multiple_of((1 - c) * HALF, HALF), HALF)

        def out_copy(i):
            g = tile_of(i)
            micro = y // 2
            return rcopy(V.at[i], out.at[micro], out_s.at[i], out_r.at[micro], (s, g))

        def own_copy(i):
            micro = y // 2
            return pltpu.make_async_copy(V.at[i], out.at[micro], out_r.at[micro])

        def strips_of(i, rim_in):
            g = tile_of(i)
            pieces = []
            for side in range(4):
                pieces.append(rim_in[4 * nb[0, side, g] + nb[1, side, g]])
            for corner in range(4, 8):
                pieces.append(rim_in[4 * nb[0, corner, g] + (nb[1, corner, g] & 2)])
            return jnp.concatenate(pieces, axis=0)

        def inside(i, into):
            z = Z[i].astype(F32)
            for h in range(2):
                for r in range(16):
                    into[i % 2, h, (r + 1) * PITCH + 1:(r + 1) * PITCH + 17, :] = (
                        z[r * 16:r * 16 + 16, h * 128:h * 128 + 128]
                    )

        def around(i, rim_in):
            frame = jnp.dot(PM[i], strips_of(i, rim_in), preferred_element_type=F32)
            for h in range(2):
                f = frame[:, h * 128:h * 128 + 128]
                pad[i % 2, h, 1:17, :] = f[0:16]
                pad[i % 2, h, pl.ds(PITCH + 17, 16, stride=PITCH), :] = f[16:32]
                pad[i % 2, h, 17 * PITCH + 1:17 * PITCH + 17, :] = f[32:48]
                pad[i % 2, h, pl.ds(PITCH, 16, stride=PITCH), :] = f[48:64]
                pad[i % 2, h, 0:1, :] = f[64:65]
                pad[i % 2, h, 17:18, :] = f[65:66]
                pad[i % 2, h, 17 * PITCH + 17:17 * PITCH + 18, :] = f[66:67]
                pad[i % 2, h, 17 * PITCH:17 * PITCH + 1, :] = f[67:68]

        def nine(i, k, source):
            total = None
            for b in range(3):
                shifted = [
                    jnp.concatenate(
                        [source[i % 2, h, r * PITCH + b:r * PITCH + b + 16, :].astype(BF16) for r in range(18)],
                        axis=0,
                    )
                    for h in range(2)
                ]
                for a in range(3):
                    q = 3 * a + b
                    lhs = jnp.concatenate([sh[a * 16:a * 16 + 256] * MB[i, q] for sh in shifted], axis=1)
                    part_sum = jnp.dot(lhs, W[k, q * C:q * C + C, :], preferred_element_type=F32)
                    total = part_sum if total is None else total + part_sum
            return total

        def finish(i, k, total, rim_out):
            half = total + 0.5 * BG[k, 0:1, :].astype(F32)
            v = (V[i].astype(F32) + half + half * jnp.tanh(half)).astype(BF16)
            V[i] = v
            nz = normed(v.astype(F32), lax.rem(k + 1, 8))
            Z[i] = nz
            keep_rim(i, rim_out, nz)

        def tile_step(i, k, rim_in, rim_out):
            around(i, rim_in)
            inside(i, pad)
            finish(i, k, nine(i, k, pad), rim_out)

        def first_inside(k):
            for i in range(2):
                inside(i, bare)
                total = nine(i, k, bare)
                for h in range(2):
                    early[i, h] = total[:, h * 128:h * 128 + 128]

        def first_frames(k, rim_in, rim_out):
            rows = []
            for i in range(2):
                chosen = jnp.dot(PMC[i], strips_of(i, rim_in), preferred_element_type=F32).astype(BF16)
                rows.append(
                    jnp.concatenate([chosen[:, 0:128] * MBC[i], chosen[:, 128:256] * MBC[i]], axis=1)
                )
            sums = [[None] * 4 for _ in range(2)]
            for q in range(9):
                mine_q = [(n, b[0]) for n, b in enumerate(BLOCKS) if b[1] == q]
                if not mine_q:
                    continue
                lhs = jnp.concatenate([rows[i][n * 16:n * 16 + 16] for i in range(2) for n, _ in mine_q], axis=0)
                got = jnp.dot(lhs, W[k, q * C:q * C + C, :], preferred_element_type=F32)
                at = 0
                for i in range(2):
                    for _, side in mine_q:
                        piece = got[at:at + 16]
                        at += 16
                        sums[i][side] = piece if sums[i][side] is None else sums[i][side] + piece
            for i in range(2):
                for h in range(2):
                    lanes = slice(h * 128, h * 128 + 128)
                    for side, where in (
                        (0, pl.ds(0, 16)), (2, pl.ds(240, 16)),
                        (3, pl.ds(0, 16, stride=16)), (1, pl.ds(15, 16, stride=16)),
                    ):
                        early[i, h, where, :] = early[i, h, where, :] + sums[i][side][:, lanes]
                finish(i, k, jnp.concatenate([early[i, 0], early[i, 1]], axis=1), rim_out)

        def deliver(i):
            g = tile_of(i)

            @pl.when(t == g)
            def _():
                own_copy(i).start()

            @pl.when(t != g)
            def _():
                out_copy(i).start()

        def layer(k, rim_in, par_in, rim_out, par_out):
            @pl.when(k > 0)
            def _():
                rcopy(W.at[k, other], W.at[k, other], x_s.at[k], x_r.at[k], partner).wait_recv()

            first_inside(k)
            for p in range(4):
                rim_copy(p, rim_in, par_in, 1 - c).wait_recv()
            first_frames(k, rim_in, rim_out)

            for p in range(4):
                if p > 0:
                    for i in (2 * p, 2 * p + 1):
                        tile_step(i, k, rim_in, rim_out)
                rim_copy(p, rim_out, par_out, c).start()
                if p == 1:
                    @pl.when(k < 7)
                    def _():
                        arrived(k + 1)
                        exchange(k + 1).start()
                if p % 2 == 1 and par_out == 0:
                    @pl.when(k == 7)
                    def _():
                        for i in range(2 * p - 2, 2 * p + 2):
                            deliver(i)

        @pl.loop(0, 4)
        def _(n):
            @pl.when(n > 0)
            def _():
                for p in range(4):
                    rim_copy(p, rim_b, 1, c).wait_send()
            layer(2 * n, rim_a, 0, rim_b, 1)
            for p in range(4):
                rim_copy(p, rim_a, 0, c).wait_send()
            layer(2 * n + 1, rim_b, 1, rim_a, 0)

        for p in range(4):
            rim_copy(p, rim_b, 1, c).wait_send()
            rim_copy(p, rim_a, 0, c).wait_send()
            rim_copy(p, rim_a, 0, 1 - c).wait_recv()
        for k in range(1, 8):
            exchange(k).wait_send()
        for n, d in enumerate(f1_dst):
            sent(d, n)
        for p in range(4):
            hub3_in(p).wait_send()
        told(f1_dst + [e3_dst])
        for i in range(8):
            @pl.when(t != tile_of(i))
            def _():
                out_copy(i).wait_send()

    for j in range(2):
        @pl.when(jnp.logical_not(is_home[j]))
        def _():
            rcopy(metric.at[0], metr.at[slots[j]], met_s.at[j], met_r.at[slots[j]], homes[j]).wait_send()
            rcopy(act.at[j], V.at[slots[j]], act_s.at[j], act_r.at[slots[j]], homes[j]).wait_send()
        rcopy(V.at[0], out.at[j], out_s.at[0], out_r.at[j], partner).wait_recv()


def local(activations, weight, conv_bias, norm_gain, metric, neighbours):
    anywhere = pl.BlockSpec(memory_space=pl.ANY)
    vmem = pl.BlockSpec(memory_space=pltpu.VMEM)
    dma = pltpu.SemaphoreType.DMA
    out = pl.pallas_call(
        kernel,
        name="sphere",
        out_shape=jax.ShapeDtypeStruct((2, C, C), BF16),
        in_specs=[pl.BlockSpec(memory_space=pltpu.SMEM), anywhere, anywhere, anywhere, vmem, vmem],
        out_specs=anywhere,
        scratch_shapes=[
            pltpu.VMEM((8, 9 * C, C), BF16),
            pltpu.VMEM((8, C, C), BF16),
            pltpu.VMEM((8, C, C), BF16),
            pltpu.VMEM((64, 16, C), BF16),
            pltpu.VMEM((64, 16, C), BF16),
            pltpu.VMEM((8, 9, C), BF16),
            pltpu.VMEM((8, 9, C, 128), BF16),
            pltpu.VMEM((8, 16, C), BF16),
            pltpu.VMEM((16, C), BF16),
            pltpu.VMEM((8, 80, 128), BF16),
            pltpu.VMEM((2, 2, 336, 128), F32),
            dma((2,)), dma((8,)), dma((2,)), dma((8,)),
            dma((3,)), dma((8,)), dma((3,)), dma((8,)),
            dma((8,)), dma((8,)),
            dma((2, 4)), dma((2, 4)), dma((8,)), dma((2,)), dma((1,)), dma((8,)), dma((4,)),
            pltpu.SemaphoreType.REGULAR,
            pltpu.VMEM((2, 2, 336, 128), F32),
            pltpu.VMEM((2, 2, C, 128), F32),
            pltpu.VMEM((2, 192, 128), BF16),
            pltpu.VMEM((2, 192, 128), BF16),
        ],
        compiler_params=pltpu.CompilerParams(
            collective_id=0, has_side_effects=True
        ),
    )(
        neighbours.transpose(0, 2, 1),
        activations.reshape(2, C, C),
        weight.reshape(9 * C, C),
        metric,
        conv_bias,
        norm_gain,
    )
    return out.reshape(2, 1, 16, 16, C)


def solution(mesh):
    in_specs = (
        P("section", "tile", None, None, None),
        P("section", None, None, None),
        P("section", None),
        P("section", None),
        P("tile", None, None),
        P(),
    )
    out_specs = P("section", "tile", None, None, None)
    return jax.shard_map(local, mesh=mesh, in_specs=in_specs, out_specs=out_specs, check_vma=False)
```

```python
import jax
import jax.numpy as jnp
from jax import lax
from jax.experimental import pallas as pl
from jax.experimental.pallas import tpu as pltpu
from jax.sharding import PartitionSpec as P

MESH = pl.DeviceIdType.MESH
C = 256
HALF = 9 * C // 2
F32, BF16 = jnp.float32, jnp.bfloat16
PITCH = 18


def rcopy(src, dst, send, recv, device):
    return pltpu.make_async_remote_copy(
        src_ref=src, dst_ref=dst, send_sem=send, recv_sem=recv, device_id=device, device_id_type=MESH
    )


def kernel(
    nb, act, weight, metric, bias, gain, out,
    W, V, Z, rim_a, rim_b, metr, MB, BG, bgs, PM, pad,
    act_s, act_r, met_s, met_r, w_s, w_r, bg_s, bg_r, x_s, x_r,
    rim_s, rim_r, out_s, out_r, loc, hub_s, hub_r, go,
    bare, early, PMC, MBC,
):
    s, t = lax.axis_index("section"), lax.axis_index("tile")
    hi, x = s // 4, lax.rem(s, 4)
    zl, y, c = t // 8, lax.rem(t // 2, 4), lax.rem(t, 2)
    even = lax.rem(y, 2) == 0
    active = jnp.logical_and(zl == 1, even)
    relay = jnp.logical_and(zl == 1, jnp.logical_not(even))
    cross1 = jnp.logical_and(zl == 0, even)
    cross2 = jnp.logical_and(zl == 0, jnp.logical_not(even))

    def sec(h, xx):
        return h * 4 + lax.rem(xx + 8, 4)

    def tid(plane, row, core):
        return plane * 8 + 2 * lax.rem(row + 4, 4) + core

    partner = (s, t + 1 - 2 * c)
    homes = [(s, 8 + zl), (s, 12 + zl)]
    is_home = [t == 8 + zl, t == 12 + zl]

    f1_dst = [(sec(hi, x - 1), t), (sec(hi, x + 1), t)]
    f2_dst = (sec(hi, x + 2), tid(1, y - 1, c))
    e3_dst = (sec(1 - hi, x + 1), t)
    hub_dst = (s, tid(1, y + 1, c))
    hub_src = (sec(1 - hi, jnp.where(x == 3, 1, x)), tid(0, y, c))
    hub_k = jnp.where(x == 3, 2, 4)
    e3_hub = (e3_dst[0], tid(0, y, c))
    hub3_src = (sec(1 - hi, x - 1), tid(1, y, c))
    hub3_dst = (s, tid(1, y, c))
    hub3_k = lax.rem(hub3_src[0] - s + 8, 8)
    near = (sec(1 - hi, x), tid(1, jnp.where(x == 3, y + 1, y), c))
    far = (sec(1 - hi, x + 2), tid(1, jnp.where(x == 1, y, y - 1), c))
    e1_dst = (sec(1 - hi, x - 1), tid(1, y, c))
    e3_src = (sec(1 - hi, x - 1), t)
    w_src = [
        (sec(hi, x + 1), t), (sec(hi, x - 1), t), (sec(hi, x + 2), tid(1, y + 1, c)), (s, tid(1, y - 1, c)), e3_src,
        (s, tid(0, y, c)), (sec(1 - hi, x + 1), tid(0, y, c)),
        (sec(1 - hi, jnp.where(x == 3, x, x + 2)), tid(0, jnp.where(x == 3, y - 1, y + 1), c)),
    ]

    barrier = pltpu.get_barrier_semaphore()

    def hello(device):
        pl.semaphore_signal(barrier, inc=1, device_id=device, device_id_type=MESH)

    for j in range(2):
        @pl.when(jnp.logical_not(is_home[j]))
        def _():
            hello(homes[j])

    @pl.when(active)
    def _():
        for i in range(8):
            @pl.when(t != c * 8 + i)
            def _():
                hello((s, c * 8 + i))
        for d in w_src + [e3_dst, e3_hub]:
            hello(d)
        hello(partner)

    @pl.when(relay)
    def _():
        for d in (f2_dst, hub_dst, hub_src):
            hello(d)

    @pl.when(cross1)
    def _():
        for d in (e1_dst, hub3_src, hub3_dst):
            hello(d)

    @pl.when(cross2)
    def _():
        hello(near)
        hello(far)

    at_home = jnp.logical_or(is_home[0], is_home[1])
    greeted = jnp.where(at_home, 1, 2) + jnp.where(relay, 3, jnp.where(active, jnp.where(c == zl, 18, 19), 3 - lax.rem(y, 2)))
    pl.semaphore_wait(barrier, greeted)

    def place(row, row0):
        rel = lax.rem(row - row0 + 4, 4)
        return jnp.where(rel == 0, 3, jnp.where(rel == 1, 1, jnp.where(rel == 2, 0, 2)))

    slots = [2 * place(y, 2 * j) + c for j in range(2)]
    for j in range(2):
        @pl.when(is_home[j])
        def _():
            pltpu.make_async_copy(metric.at[0], metr.at[slots[j]], met_r.at[slots[j]]).start()
            pltpu.make_async_copy(act.at[j], V.at[slots[j]], act_r.at[slots[j]]).start()

        @pl.when(jnp.logical_not(is_home[j]))
        def _():
            rcopy(metric.at[0], metr.at[slots[j]], met_s.at[j], met_r.at[slots[j]], homes[j]).start()
            rcopy(act.at[j], V.at[slots[j]], act_s.at[j], act_r.at[slots[j]], homes[j]).start()

    bgs[0:8] = jnp.broadcast_to(bias[...], (8, C))
    bgs[8:16] = jnp.broadcast_to(gain[...], (8, C))

    mine = pl.ds(pl.multiple_of(c * HALF, HALF), HALF)

    def stream(device, n):
        k = lax.rem(s - device[0] + 8, 8)
        return rcopy(weight.at[mine], W.at[k, mine], w_s.at[n], w_r.at[k], device)

    def begin(device, n):
        stream(device, n).start()

    def sent(device, n):
        stream(device, n).wait_send()

    def lines(device, n):
        k = lax.rem(s - device[0] + 8, 8)
        return rcopy(bgs, BG.at[k], bg_s.at[n], bg_r.at[k], device)

    def tell(devices):
        for n, d in enumerate(devices):
            lines(d, n).start()

    def told(devices):
        for n, d in enumerate(devices):
            lines(d, n).wait_send()

    def arrived(k):
        rcopy(weight.at[mine], W.at[k, mine], w_s.at[0], w_r.at[k], partner).wait_recv()

    PART = HALF // 4

    def part(p, n=1):
        return pl.ds(pl.multiple_of(c * HALF + p * PART, 16), n * PART)

    def hub_in(p, device, n):
        k = lax.rem(s - device[0] + 8, 8)
        return rcopy(weight.at[part(p)], W.at[k, part(p)], hub_s.at[n + p], hub_r.at[p], device)

    def hub_on(p):
        return rcopy(W.at[hub_k, part(p)], W.at[hub_k, part(p)], hub_s.at[p], w_r.at[hub_k], hub_dst)

    def hub3_in(p):
        k = lax.rem(s - e3_hub[0] + 8, 8)
        return rcopy(weight.at[part(p)], W.at[k, part(p)], hub_s.at[4 + p], hub_r.at[p], e3_hub)

    def hub3_on(p):
        return rcopy(W.at[hub3_k, part(p)], W.at[hub3_k, part(p)], hub_s.at[p], w_r.at[hub3_k], hub3_dst)

    @pl.when(relay)
    def _():
        tell((f2_dst,))

        @pl.when(x >= 2)
        def _():
            begin(f2_dst, 0)
        for p in range(4):
            rcopy(weight.at[part(p)], W.at[hub_k, part(p)], hub_s.at[p], hub_r.at[p], f2_dst).wait_recv()
            hub_on(p).start()
        rcopy(bgs, BG.at[hub_k], bg_s.at[2], bg_r.at[hub_k], f2_dst).wait_recv()
        hub_line = rcopy(BG.at[hub_k], BG.at[hub_k], bg_s.at[2], bg_r.at[hub_k], hub_dst)
        hub_line.start()

        @pl.when(x < 2)
        def _():
            begin(f2_dst, 0)
        sent(f2_dst, 0)
        for p in range(4):
            hub_on(p).wait_send()
        hub_line.wait_send()
        told((f2_dst,))

    @pl.when(cross1)
    def _():
        tell((e1_dst,))

        @pl.when(x == 0)
        def _():
            begin(e1_dst, 0)
        pl.semaphore_wait(go, 1)

        @pl.when(x != 0)
        def _():
            begin(e1_dst, 0)
        for p in range(4):
            rcopy(weight.at[part(p)], W.at[hub3_k, part(p)], hub_s.at[p], hub_r.at[p], e1_dst).wait_recv()
            hub3_on(p).start()
        sent(e1_dst, 0)
        for p in range(4):
            hub3_on(p).wait_send()
        told((e1_dst,))

    def halves(n):
        k = lax.rem(s - far[0] + 8, 8)
        return rcopy(weight.at[part(2 * n, 2)], W.at[k, part(2 * n, 2)], w_s.at[2 * n], w_r.at[k], far)

    @pl.when(cross2)
    def _():
        tell((near, far))

        @pl.when(x == 3)
        def _():
            halves(0).start()
            halves(0).wait_send()
            begin(near, 1)
            sent(near, 1)
            halves(1).start()
            halves(1).wait_send()

        @pl.when(x == 1)
        def _():
            for p in range(4):
                hub_in(p, far, 4).start()

        @pl.when(x == 0)
        def _():
            begin(far, 0)

        @pl.when(x != 3)
        def _():
            for p in range(4):
                hub_in(p, near, 0).start()
            for p in range(4):
                hub_in(p, near, 0).wait_send()

        @pl.when(x == 1)
        def _():
            for p in range(4):
                hub_in(p, far, 4).wait_send()

        @pl.when(x == 2)
        def _():
            begin(far, 0)

        @pl.when(jnp.logical_or(x == 0, x == 2))
        def _():
            sent(far, 0)
        told((near, far))

    @pl.when(active)
    def _():
        tell(f1_dst + [e3_dst])
        for p in range(4):
            hub3_in(p).start()
        for n, d in enumerate(f1_dst):
            begin(d, n)
        own_w = pltpu.make_async_copy(weight, W.at[0], loc.at[0])
        own_w.start()
        BG[0] = bgs[...]

        def tile_of(i):
            pos = i // 2
            if isinstance(i, int):
                rel = (2, 1, 3, 0)[pos]
            else:
                rel = jnp.where(pos == 0, 2, jnp.where(pos == 1, 1, jnp.where(pos == 2, 3, 0)))
            return c * 8 + 2 * lax.rem(y + rel, 4) + (i % 2 if isinstance(i, int) else lax.rem(i, 2))

        @pl.loop(0, 8)
        def _(i):
            g = tile_of(i)
            row = lax.broadcasted_iota(jnp.int32, (16, 128), 0)
            col = lax.broadcasted_iota(jnp.int32, (16, 128), 1)
            for side in range(4):
                flip = nb[2, side, g]
                want = side * 16 + row + flip * (15 - 2 * row)
                PM[i, side * 16:side * 16 + 16, :] = jnp.where(col == want, 1.0, 0.0).astype(BF16)
            want = jnp.zeros((16, 128), jnp.int32) - 1
            for corner in range(4):
                which = nb[1, 4 + corner, g]
                last = 15 * (((which + 1) >> 1) & 1)
                want = jnp.where(row == corner, 64 + corner * 16 + last, want)
            PM[i, 64:80, :] = jnp.where(col == want, 1.0, 0.0).astype(BF16)

        @pl.loop(0, 8)
        def _(i):
            rcopy(metric.at[0], metr.at[i], met_s.at[0], met_r.at[i], partner).wait_recv()
            for q in range(9):
                line = jnp.broadcast_to(0.5 * metr[i, q:q + 1, :].astype(F32), (128, C))
                MB[i, q] = line.T.astype(BF16)

        bare[...] = jnp.zeros_like(bare)
        BLOCKS = [
            (0, 0, -1, 0), (0, 1, 0, None), (0, 2, 1, 1), (2, 6, -1, 3), (2, 7, 0, None), (2, 8, 1, 2),
            (3, 0, -1, None), (3, 3, 0, None), (3, 6, 1, None), (1, 2, -1, None), (1, 5, 0, None), (1, 8, 1, None),
        ]
        for i in range(2):
            g = tile_of(i)
            row = lax.broadcasted_iota(jnp.int32, (16, 128), 0)
            col = lax.broadcasted_iota(jnp.int32, (16, 128), 1)
            for n, (side, q, shift, corner) in enumerate(BLOCKS):
                m = row + shift
                flip = nb[2, side, g]
                want = side * 16 + m + flip * (15 - 2 * m)
                beyond = -1
                if corner is not None:
                    which = nb[1, 4 + corner, g]
                    beyond = 64 + corner * 16 + 15 * (((which + 1) >> 1) & 1)
                want = jnp.where(jnp.logical_or(m < 0, m > 15), beyond, want)
                here = slice(n * 16, n * 16 + 16)
                PMC[i, here, :] = jnp.where(col == want, 1.0, 0.0).astype(BF16)
                cube = MB[i, q].astype(F32).reshape(16, 16, 128)
                edge = (cube[0], cube[:, 15], cube[15], cube[:, 0])[side]
                MBC[i, here, :] = edge.astype(BF16)

        def normed(values, k):
            mean_sq = jnp.mean(values * values, axis=-1, keepdims=True)
            return (values * lax.rsqrt(mean_sq + 1e-05) * BG[k, 8:9, :].astype(F32)).astype(BF16)

        def keep_rim(i, rim, z):
            g = tile_of(i)
            cube = z.astype(F32).reshape(16, 16, C)
            rim[4 * g] = z[0:16]
            rim[4 * g + 1] = cube[:, 15, :].astype(BF16)
            rim[4 * g + 2] = z[240:256]
            rim[4 * g + 3] = cube[:, 0, :].astype(BF16)

        def rim_copy(p, rim, par, who):
            own = pl.ds(4 * (tile_of(2 * p) + 8 * (who - c)), 8)
            return rcopy(rim.at[own], rim.at[own], rim_s.at[par, p], rim_r.at[par, p], partner)

        @pl.loop(0, 4)
        def _(p):
            for i in (2 * p, 2 * p + 1):
                rcopy(act.at[0], V.at[i], act_s.at[0], act_r.at[i], partner).wait_recv()
                z = normed(V[i].astype(F32), 0)
                Z[i] = z
                keep_rim(i, rim_a, z)
            rim_copy(p, rim_a, 0, c).start()

            @pl.when(jnp.logical_and(p == 3, c == 0))
            def _():
                for core in range(2):
                    pl.semaphore_signal(go, inc=1, device_id=(s, tid(0, y, core)), device_id_type=MESH)

        own_w.wait()
        for k in range(1, 8):
            rcopy(bgs, BG.at[k], bg_s.at[0], bg_r.at[k], partner).wait_recv()

        def exchange(k):
            return rcopy(W.at[k, mine], W.at[k, mine], x_s.at[k], x_r.at[k], partner)

        other = pl.ds(pl.multiple_of((1 - c) * HALF, HALF), HALF)

        def out_copy(i):
            g = tile_of(i)
            micro = y // 2
            return rcopy(V.at[i], out.at[micro], out_s.at[i], out_r.at[micro], (s, g))

        def own_copy(i):
            micro = y // 2
            return pltpu.make_async_copy(V.at[i], out.at[micro], out_r.at[micro])

        def strips_of(i, rim_in):
            g = tile_of(i)
            pieces = []
            for side in range(4):
                pieces.append(rim_in[4 * nb[0, side, g] + nb[1, side, g]])
            for corner in range(4, 8):
                pieces.append(rim_in[4 * nb[0, corner, g] + (nb[1, corner, g] & 2)])
            return jnp.concatenate(pieces, axis=0)

        def inside(i, into):
            z = Z[i].astype(F32)
            for h in range(2):
                for r in range(16):
                    into[i % 2, h, (r + 1) * PITCH + 1:(r + 1) * PITCH + 17, :] = (
                        z[r * 16:r * 16 + 16, h * 128:h * 128 + 128]
                    )

        def around(i, rim_in):
            frame = jnp.dot(PM[i], strips_of(i, rim_in), preferred_element_type=F32)
            for h in range(2):
                f = frame[:, h * 128:h * 128 + 128]
                pad[i % 2, h, 1:17, :] = f[0:16]
                pad[i % 2, h, pl.ds(PITCH + 17, 16, stride=PITCH), :] = f[16:32]
                pad[i % 2, h, 17 * PITCH + 1:17 * PITCH + 17, :] = f[32:48]
                pad[i % 2, h, pl.ds(PITCH, 16, stride=PITCH), :] = f[48:64]
                pad[i % 2, h, 0:1, :] = f[64:65]
                pad[i % 2, h, 17:18, :] = f[65:66]
                pad[i % 2, h, 17 * PITCH + 17:17 * PITCH + 18, :] = f[66:67]
                pad[i % 2, h, 17 * PITCH:17 * PITCH + 1, :] = f[67:68]

        def nine(i, k, source):
            total = None
            for b in range(3):
                shifted = [
                    jnp.concatenate(
                        [source[i % 2, h, r * PITCH + b:r * PITCH + b + 16, :].astype(BF16) for r in range(18)],
                        axis=0,
                    )
                    for h in range(2)
                ]
                for a in range(3):
                    q = 3 * a + b
                    lhs = jnp.concatenate([sh[a * 16:a * 16 + 256] * MB[i, q] for sh in shifted], axis=1)
                    part_sum = jnp.dot(lhs, W[k, q * C:q * C + C, :], preferred_element_type=F32)
                    total = part_sum if total is None else total + part_sum
            return total

        def finish(i, k, total, rim_out):
            half = total + 0.5 * BG[k, 0:1, :].astype(F32)
            v = (V[i].astype(F32) + half + half * jnp.tanh(half)).astype(BF16)
            V[i] = v
            nz = normed(v.astype(F32), lax.rem(k + 1, 8))
            Z[i] = nz
            keep_rim(i, rim_out, nz)

        def tile_step(i, k, rim_in, rim_out):
            around(i, rim_in)
            inside(i, pad)
            finish(i, k, nine(i, k, pad), rim_out)

        def first_inside(k):
            for i in range(2):
                inside(i, bare)
                total = nine(i, k, bare)
                for h in range(2):
                    early[i, h] = total[:, h * 128:h * 128 + 128]

        def first_frames(k, rim_in, rim_out):
            rows = []
            for i in range(2):
                chosen = jnp.dot(PMC[i], strips_of(i, rim_in), preferred_element_type=F32).astype(BF16)
                rows.append(
                    jnp.concatenate([chosen[:, 0:128] * MBC[i], chosen[:, 128:256] * MBC[i]], axis=1)
                )
            sums = [[None] * 4 for _ in range(2)]
            for q in range(9):
                mine_q = [(n, b[0]) for n, b in enumerate(BLOCKS) if b[1] == q]
                if not mine_q:
                    continue
                lhs = jnp.concatenate([rows[i][n * 16:n * 16 + 16] for i in range(2) for n, _ in mine_q], axis=0)
                got = jnp.dot(lhs, W[k, q * C:q * C + C, :], preferred_element_type=F32)
                at = 0
                for i in range(2):
                    for _, side in mine_q:
                        piece = got[at:at + 16]
                        at += 16
                        sums[i][side] = piece if sums[i][side] is None else sums[i][side] + piece
            for i in range(2):
                for h in range(2):
                    lanes = slice(h * 128, h * 128 + 128)
                    for side, where in (
                        (0, pl.ds(0, 16)), (2, pl.ds(240, 16)),
                        (3, pl.ds(0, 16, stride=16)), (1, pl.ds(15, 16, stride=16)),
                    ):
                        early[i, h, where, :] = early[i, h, where, :] + sums[i][side][:, lanes]
                finish(i, k, jnp.concatenate([early[i, 0], early[i, 1]], axis=1), rim_out)

        def deliver(i):
            g = tile_of(i)

            @pl.when(t == g)
            def _():
                own_copy(i).start()

            @pl.when(t != g)
            def _():
                out_copy(i).start()

        def layer(k, rim_in, par_in, rim_out, par_out):
            @pl.when(k > 0)
            def _():
                rcopy(W.at[k, other], W.at[k, other], x_s.at[k], x_r.at[k], partner).wait_recv()

            first_inside(k)
            for p in range(4):
                rim_copy(p, rim_in, par_in, 1 - c).wait_recv()
            first_frames(k, rim_in, rim_out)

            for p in range(4):
                if p > 0:
                    for i in (2 * p, 2 * p + 1):
                        tile_step(i, k, rim_in, rim_out)
                rim_copy(p, rim_out, par_out, c).start()
                if p == 0:
                    @pl.when(k < 7)
                    def _():
                        arrived(k + 1)
                        exchange(k + 1).start()
                if p % 2 == 1 and par_out == 0:
                    @pl.when(k == 7)
                    def _():
                        for i in range(2 * p - 2, 2 * p + 2):
                            deliver(i)

        @pl.loop(0, 4)
        def _(n):
            @pl.when(n > 0)
            def _():
                for p in range(4):
                    rim_copy(p, rim_b, 1, c).wait_send()
            layer(2 * n, rim_a, 0, rim_b, 1)
            for p in range(4):
                rim_copy(p, rim_a, 0, c).wait_send()
            layer(2 * n + 1, rim_b, 1, rim_a, 0)

        for p in range(4):
            rim_copy(p, rim_b, 1, c).wait_send()
            rim_copy(p, rim_a, 0, c).wait_send()
            rim_copy(p, rim_a, 0, 1 - c).wait_recv()
        for k in range(1, 8):
            exchange(k).wait_send()
        for n, d in enumerate(f1_dst):
            sent(d, n)
        for p in range(4):
            hub3_in(p).wait_send()
        told(f1_dst + [e3_dst])
        for i in range(8):
            @pl.when(t != tile_of(i))
            def _():
                out_copy(i).wait_send()

    for j in range(2):
        @pl.when(jnp.logical_not(is_home[j]))
        def _():
            rcopy(metric.at[0], metr.at[slots[j]], met_s.at[j], met_r.at[slots[j]], homes[j]).wait_send()
            rcopy(act.at[j], V.at[slots[j]], act_s.at[j], act_r.at[slots[j]], homes[j]).wait_send()
        rcopy(V.at[0], out.at[j], out_s.at[0], out_r.at[j], partner).wait_recv()


def local(activations, weight, conv_bias, norm_gain, metric, neighbours):
    anywhere = pl.BlockSpec(memory_space=pl.ANY)
    vmem = pl.BlockSpec(memory_space=pltpu.VMEM)
    dma = pltpu.SemaphoreType.DMA
    out = pl.pallas_call(
        kernel,
        name="sphere",
        out_shape=jax.ShapeDtypeStruct((2, C, C), BF16),
        in_specs=[pl.BlockSpec(memory_space=pltpu.SMEM), anywhere, anywhere, anywhere, vmem, vmem],
        out_specs=anywhere,
        scratch_shapes=[
            pltpu.VMEM((8, 9 * C, C), BF16),
            pltpu.VMEM((8, C, C), BF16),
            pltpu.VMEM((8, C, C), BF16),
            pltpu.VMEM((64, 16, C), BF16),
            pltpu.VMEM((64, 16, C), BF16),
            pltpu.VMEM((8, 9, C), BF16),
            pltpu.VMEM((8, 9, C, 128), BF16),
            pltpu.VMEM((8, 16, C), BF16),
            pltpu.VMEM((16, C), BF16),
            pltpu.VMEM((8, 80, 128), BF16),
            pltpu.VMEM((2, 2, 336, 128), F32),
            dma((2,)), dma((8,)), dma((2,)), dma((8,)),
            dma((3,)), dma((8,)), dma((3,)), dma((8,)),
            dma((8,)), dma((8,)),
            dma((2, 4)), dma((2, 4)), dma((8,)), dma((2,)), dma((1,)), dma((8,)), dma((4,)),
            pltpu.SemaphoreType.REGULAR,
            pltpu.VMEM((2, 2, 336, 128), F32),
            pltpu.VMEM((2, 2, C, 128), F32),
            pltpu.VMEM((2, 192, 128), BF16),
            pltpu.VMEM((2, 192, 128), BF16),
        ],
        compiler_params=pltpu.CompilerParams(
            collective_id=0, has_side_effects=True
        ),
    )(
        neighbours.transpose(0, 2, 1),
        activations.reshape(2, C, C),
        weight.reshape(9 * C, C),
        metric,
        conv_bias,
        norm_gain,
    )
    return out.reshape(2, 1, 16, 16, C)


def solution(mesh):
    in_specs = (
        P("section", "tile", None, None, None),
        P("section", None, None, None),
        P("section", None),
        P("section", None),
        P("tile", None, None),
        P(),
    )
    out_specs = P("section", "tile", None, None, None)
    return jax.shard_map(local, mesh=mesh, in_specs=in_specs, out_specs=out_specs, check_vma=False)
```
